32 devices in a mesh: grp: 2 (over y), mesh: 4 (over z), tm: 2 (over x), rep: 2 (over core).
Axes of the slice: x: 2, y: 2, z: 4, core: 2. Of those that a mesh axis runs over, the one named last changes fastest.
Arguments:
- right_side: float32 [4, 128, 64, 128], P(('grp', 'tm'), ('mesh', 'rep')), parts along dimension 0, may hold values from -25 to 25
- kappa_sq: float32 [256, 64], P(('grp', 'mesh', 'rep')), parts along dimension 0, may hold values from 0.25 to 4
- time_coupling: float32 [2], P('grp'), parts along dimension 0, may hold values from 0.15 to 0.45
- near_stiffness: float32 [128, 64, 384], P(('mesh', 'rep')), may hold values from -0.16 to 0.16, as said below
- far_stiffness: float32 [8, 64, 1536], P(('mesh', 'rep')), may hold values from -0.16 to 0.16, as said below
- near_columns: int32 [128, 6], P(('mesh', 'rep')), may hold values from 0 to 15, as said below
- face_blocks: int32 [8, 6, 4], P(('mesh', 'rep')), may hold values from 0 to 15, as said below
- face_counts: int32 [8, 6], P(('mesh', 'rep')), may hold values from 0 to 4, as said below
Outputs:
- solution_field: float32 [4, 128, 64, 128], P(('grp', 'tm'), ('mesh', 'rep')), parts along dimension 0
- residual: float32 [4, 128, 64, 128], P(('grp', 'tm'), ('mesh', 'rep')), parts along dimension 0
The draws below stay inside these ranges and needn't reach their ends.
There are 2 independent parts, one for each index of `grp`. The reference program is written for one: setup_inputs(seed, part) draws one part's arguments, and reference() takes and returns one part's arrays. A program takes and returns all parts, laid end to end along the dimension named above; an argument that names none is the same for every part. Nothing has to cross between parts.
Inputs may be any that keep to these rules, and one draw needn't show every extreme that they name: face_counts[n(p, e), e'] = face_counts[p, e]; every partition sends 4 blocks toward at least one direction. `face_blocks`: the 4 blocks of one partition and direction are distinct. `near_columns`: for j < 3, slot 2j over the block rows of a partition is a permutation of its local blocks and slot 2j + 1 is the inverse permutation. `near_stiffness`: for j < 3, the block in slot 2j + 1 of block row b is the transpose of the block in slot 2j of the block row that slot 2j + 1 of b names. `far_stiffness`: G[n(p, e), e' * 4 + f] is the transpose of G[p, e * 4 + f].
All inputs are finite; a program needn't handle non-finite values.
Results may differ from the reference program's by a relative error of at most 0.00016.
Values sent between devices are 32-bit elements; how exact they have to be, the bound alone decides.
No kernel may reach another device: no remote copies, remote signals or barrier semaphores. Data moves between devices by JAX's collectives and lax.ppermute only.
A program may use at most 64 MiB of HBM per device.

```python
import math
import jax
import jax.numpy as jnp
from jax import lax

BLK = 64
NB_DEV = 16
PROBES = 128
K_LOC = 6
FACE = 4
ITERS = 2
NPART = 8
STRIDE = 3
NBLOCKS = 128
HOURS = 2


stiff_scale = 0.04


stiff_bound = 0.16


def near_pattern(key):
    pairs = K_LOC // 2
    scores = jax.random.randint(jax.random.fold_in(key, 53), (pairs, NPART, NB_DEV), 0, 2 ** 20)
    scores = scores * NB_DEV + jnp.arange(NB_DEV, dtype=jnp.int32)[None, None, :]
    forward = jnp.argsort(scores, axis=-1).astype(jnp.int32)
    backward = jnp.argsort(forward, axis=-1).astype(jnp.int32)
    return (forward, backward)


def face_layout(key):
    base_key = jax.random.fold_in(key, 71)
    key_count, key_full, key_blocks = jax.random.split(base_key, 3)
    edge_count = jax.random.randint(key_count, (NPART, 3), 0, FACE + 1)
    full_dir = jax.random.randint(key_full, (NPART,), 0, 3)
    edge_count = jnp.where(jnp.arange(3)[None, :] == full_dir[:, None], FACE, edge_count)
    plus_offsets = jnp.array([1, 2, STRIDE], dtype=jnp.int32)
    parts = jnp.arange(NPART, dtype=jnp.int32)
    lower = (parts[:, None] - plus_offsets[None, :]) % NPART
    minus_count = edge_count[lower, jnp.arange(3)[None, :]]
    counts = jnp.stack([edge_count, minus_count], axis=-1).reshape(NPART, 6)
    scores = jax.random.randint(key_blocks, (NPART, 6, NB_DEV), 0, 2 ** 20)
    scores = scores * NB_DEV + jnp.arange(NB_DEV, dtype=jnp.int32)[None, None, :]
    blocks = lax.top_k(scores, FACE)[1]
    return (counts.astype(jnp.int32), blocks.astype(jnp.int32))


def draw_near_columns(key, part):
    forward, backward = near_pattern(key)
    columns = jnp.stack([forward, backward], axis=-1)
    columns = jnp.transpose(columns, (1, 2, 0, 3))
    return columns.reshape(NBLOCKS, K_LOC).astype(jnp.int32)


def draw_near_stiffness(key, part):
    forward, backward = near_pattern(key)
    pairs = K_LOC // 2
    shape = (pairs, NPART, NB_DEV, BLK, BLK)
    value_key = jax.random.fold_in(key, 59)
    values = jnp.clip(jax.random.normal(value_key, shape, jnp.float32) * stiff_scale, -stiff_bound, stiff_bound)
    mirrored = values[jnp.arange(pairs)[:, None, None], jnp.arange(NPART)[None, :, None], backward]
    mirrored = jnp.swapaxes(mirrored, 3, 4)
    both = jnp.stack([values, mirrored], axis=3)
    both = jnp.transpose(both, (1, 2, 4, 0, 3, 5))
    return both.reshape(NBLOCKS, BLK, K_LOC * BLK).astype(jnp.float32)


def draw_far_stiffness(key, part):
    shape = (NPART, 3, FACE, BLK, BLK)
    value_key = jax.random.fold_in(key, 83)
    values = jnp.clip(jax.random.normal(value_key, shape, jnp.float32) * stiff_scale, -stiff_bound, stiff_bound)
    plus_offsets = jnp.array([1, 2, STRIDE], dtype=jnp.int32)
    parts = jnp.arange(NPART, dtype=jnp.int32)
    lower = (parts[:, None] - plus_offsets[None, :]) % NPART
    mirrored = values[lower, jnp.arange(3)[None, :]]
    mirrored = jnp.swapaxes(mirrored, 3, 4)
    blocks = jnp.stack([values, mirrored], axis=2).reshape(NPART, 6, FACE, BLK, BLK)
    blocks = jnp.transpose(blocks, (0, 3, 1, 2, 4))
    return blocks.reshape(NPART, BLK, 6 * FACE * BLK).astype(jnp.float32)


def draw_face_counts(key, part):
    counts, blocks = face_layout(key)
    return counts


def draw_face_blocks(key, part):
    counts, blocks = face_layout(key)
    return blocks


def draw_right_side(key, part):
    key_main = jax.random.fold_in(jax.random.fold_in(key, 41), 0)
    hour_frac = jnp.arange(HOURS, dtype=jnp.float32) / max(HOURS - 1, 1)
    block_frac = jnp.arange(NBLOCKS, dtype=jnp.float32) / max(NBLOCKS - 1, 1)
    scaling = 3.0 ** (0.5 * hour_frac[:, None, None, None] + 0.5 * block_frac[None, :, None, None])
    shape = (HOURS, NBLOCKS, BLK, PROBES)
    base_values = jnp.clip(jax.random.normal(key_main, shape, jnp.float32), -5.0, 5.0)
    return (base_values * scaling).astype(jnp.float32)


def shard_levels(stream_key, dims, cuts, low, largest):
    factor_of, own = 1.0, jax.random.fold_in(stream_key, 6)
    for dim, shards_of in cuts:
        heights = jnp.exp(jax.random.uniform(jax.random.fold_in(own, dim), (shards_of,), jnp.float32, low / len(cuts), largest / len(cuts)))
        factor_of = factor_of * jnp.repeat(heights, dims[dim] // shards_of).reshape([-1 if axis == dim else 1 for axis in range(len(dims))])
    return factor_of


def setup_inputs(seed: int = 0, part: int = 0) -> dict:
    streams_of = jax.random.split(jax.random.key(seed), 9)
    part_keys = jax.random.split(jax.random.fold_in(streams_of[8], part), 9)
    right_side = draw_right_side(jax.random.fold_in(jax.random.fold_in(streams_of[8], part), 71), part)
    kappa_sq = jnp.clip(jnp.exp(math.log(4.0) - 2.7725887 * jax.random.uniform(part_keys[1], (NBLOCKS, BLK), jnp.float32) ** shard_levels(part_keys[1], (NBLOCKS, BLK), ((0, 8),), -0.2, 0.2)), 0.25, 4.0)
    time_coupling = jnp.clip(jax.random.uniform(part_keys[2], (1,), jnp.float32, 0.15, 0.45), 0.15, 0.45)
    near_stiffness = draw_near_stiffness(jax.random.fold_in(streams_of[8], 71), part)
    far_stiffness = draw_far_stiffness(jax.random.fold_in(streams_of[8], 71), part)
    near_columns = draw_near_columns(jax.random.fold_in(streams_of[8], 71), part)
    face_blocks = draw_face_blocks(jax.random.fold_in(streams_of[8], 71), part)
    face_counts = draw_face_counts(jax.random.fold_in(streams_of[8], 71), part)
    return dict(right_side=right_side, kappa_sq=kappa_sq, time_coupling=time_coupling, near_stiffness=near_stiffness, far_stiffness=far_stiffness, near_columns=near_columns, face_blocks=face_blocks, face_counts=face_counts)


def spatial_hour(vector, kappa_sq, near_stiffness, far_stiffness, near_columns, face_blocks, face_counts):
    owners = (jnp.arange(NBLOCKS) // NB_DEV).astype(jnp.int32)
    near_index = (owners[:, None] * NB_DEV + near_columns).astype(jnp.int32)
    nearby = vector[near_index.reshape(-1)].reshape(NBLOCKS, K_LOC * BLK, PROBES)
    parts = jnp.arange(NPART, dtype=jnp.int32)
    offsets = jnp.array([1, -1, 2, -2, STRIDE, -STRIDE], dtype=jnp.int32)
    opposite = jnp.array([1, 0, 3, 2, 5, 4], dtype=jnp.int32)
    sender_index = (parts[:, None, None] * NB_DEV + face_blocks).astype(jnp.int32)
    active = (jnp.arange(FACE, dtype=jnp.int32)[None, None, :] < face_counts[:, :, None]).astype(vector.dtype)
    sent = vector[sender_index.reshape(-1)].reshape(NPART, 6, FACE, BLK, PROBES) * active[:, :, :, None, None]
    source = ((parts[:, None] + offsets[None, :]) % NPART).astype(jnp.int32)
    received = sent[source, opposite[None, :]].reshape(NPART, 6 * FACE, BLK, PROBES)
    blocks = far_stiffness.reshape(NPART, BLK, 6 * FACE, BLK)
    far_terms = jnp.einsum("piqk,pqkx->pqix", blocks, received, precision=lax.Precision.HIGHEST)
    result = (3.0 + kappa_sq)[:, :, None] * vector
    result = result + jnp.einsum("nik,nkp->nip", near_stiffness, nearby, precision=lax.Precision.HIGHEST)
    result = result.at[sender_index.reshape(-1)].add(far_terms.reshape(NPART * 6 * FACE, BLK, PROBES))
    return result


def operate(vector, kappa_sq, time_coupling, near_stiffness, far_stiffness, near_columns, face_blocks, face_counts):
    spatial = lax.map(lambda hourly: spatial_hour(hourly, kappa_sq, near_stiffness, far_stiffness, near_columns, face_blocks, face_counts), vector)
    padded = jnp.pad(spatial, ((1, 1), (0, 0), (0, 0), (0, 0)))
    return spatial - time_coupling[0] * (padded[:-2] + padded[2:])


def reference(right_side, kappa_sq, time_coupling, near_stiffness, far_stiffness, near_columns, face_blocks, face_counts):
    solution_field = jnp.zeros_like(right_side)
    residual = right_side
    direction = right_side
    norm_now = jnp.sum(residual * residual, axis=(0, 1, 2))
    for iteration in range(ITERS):
        applied = operate(direction, kappa_sq, time_coupling, near_stiffness, far_stiffness, near_columns, face_blocks, face_counts)
        step_size = norm_now / jnp.sum(direction * applied, axis=(0, 1, 2))
        solution_field = solution_field + step_size * direction
        residual = residual - step_size * applied
        norm_next = jnp.sum(residual * residual, axis=(0, 1, 2))
        direction = residual + (norm_next / norm_now) * direction
        norm_now = norm_next
    return solution_field, residual
```

```python
import functools

import jax
import jax.numpy as jnp
from jax import lax
from jax.experimental import pallas as pl
from jax.experimental.pallas import tpu as pltpu
from jax.sharding import PartitionSpec as P

SPACE = ("mesh", "rep")
F32 = jnp.float32
BF16 = jnp.bfloat16


def vmem():
    return pl.BlockSpec(memory_space=pltpu.VMEM)


def smem():
    return pl.BlockSpec(memory_space=pltpu.SMEM)


def struct(*shape, dtype=F32):
    return jax.ShapeDtypeStruct(shape, dtype)


def call(body, outs, ins, *args):
    return pl.pallas_call(
        body,
        out_shape=outs,
        in_specs=ins,
        out_specs=jax.tree.map(lambda _: vmem(), outs),
        compiler_params=pltpu.CompilerParams(vmem_limit_bytes=48 << 20),
    )(*args)


def halves(value):
    high = value.astype(BF16)
    return high, (value - high.astype(F32)).astype(BF16)


def triple_left(value):
    high, low = halves(value)
    return jnp.concatenate([high, low, high], axis=1)


def triple_right(value):
    high, low = halves(value)
    return jnp.concatenate([high, high, low], axis=0)


def product(left, right):
    return jnp.dot(triple_left(left), triple_right(right), preferred_element_type=F32)


def pack_body(faces, field, *outs):
    for e, out in enumerate(outs):
        for f in range(out.shape[0]):
            out[f] = field[faces[0, f, e]]


def near_body(columns, kappa, stiffness, field, out, high, low, diagonal):
    blocks, width, _ = field.shape
    slots = columns.shape[0]
    diagonal[...] = jnp.transpose(kappa[...])
    for b in range(blocks):
        high[b], low[b] = halves(field[b])
    for b in range(blocks):
        total = (3.0 + diagonal[:, b : b + 1]) * field[b]
        index = [columns[k, b] for k in range(slots)]
        highs = jnp.concatenate([high[i] for i in index], axis=0)
        lows = jnp.concatenate([low[i] for i in index], axis=0)
        left_high, left_low = halves(stiffness[b])
        total += jnp.dot(left_high, highs, preferred_element_type=F32)
        total += jnp.dot(left_low, highs, preferred_element_type=F32)
        total += jnp.dot(left_high, lows, preferred_element_type=F32)
        out[b] = total


def near(columns, kappa, stiffness, field):
    return pl.pallas_call(
        near_body,
        out_shape=struct(*field.shape),
        in_specs=[smem(), vmem(), vmem(), vmem()],
        out_specs=vmem(),
        scratch_shapes=[
            pltpu.VMEM(field.shape, BF16),
            pltpu.VMEM(field.shape, BF16),
            pltpu.VMEM((kappa.shape[1], kappa.shape[0]), F32),
        ],
        compiler_params=pltpu.CompilerParams(vmem_limit_bytes=48 << 20),
    )(columns, kappa, stiffness, field)


def far_body(headings, slots, pack, faces, counts, stiffness, start, *refs):
    arrived, (out, *packed) = refs[:headings], refs[headings:]
    width = start.shape[1]
    out[...] = start[...]
    for e in range(headings):
        for f in range(slots):

            @pl.when(f < counts[0, e])
            def _(e=e, f=f):
                q = e * slots + f
                block = faces[0, f, e]
                left = stiffness[0, :, q * width : (q + 1) * width]
                out[block] += product(left, arrived[e][f])

    if pack:
        pack_body(faces, out, *packed)


def exchange(outgoing, offsets):
    count = lax.axis_size(SPACE)
    arrived = [None] * len(offsets)
    for e in sorted(range(len(offsets)), key=lambda e: -abs(offsets[e])):
        route = [(i, (i + offsets[e]) % count) for i in range(count)]
        arrived[e ^ 1] = lax.ppermute(outgoing[e], SPACE, route)
    return arrived


def rotations(value, axes):
    count = lax.axis_size(axes)
    return [
        lax.ppermute(value, axes, [(i, (i + d) % count) for i in range(count)])
        for d in range(1, count)
    ]


def total_over(value, axes):
    if lax.axis_size(axes) > 4:
        return lax.psum(value, axes)
    return functools.reduce(jnp.add, [value, *rotations(value, axes)])


def hour_rows(coupling, hour, hours, power):
    row = [jnp.where(hour == s, 1.0, 0.0) for s in range(hours)]
    for _ in range(power):
        edge = [0.0, *row, 0.0]
        row = [edge[s + 1] - coupling * (edge[s] + edge[s + 2]) for s in range(hours)]
    return [
        functools.reduce(
            jnp.add,
            [
                jnp.where(lax.rem(hour + hours - d, hours) == s, row[s], 0.0)
                for s in range(hours)
            ],
        )
        for d in range(hours)
    ]


def mix(weights, fields, b):
    return functools.reduce(jnp.add, [w * field[b] for w, field in zip(weights, fields)])


def moments_body(hours, coupling, hour, right, second, *refs):
    first, out = refs[:hours], refs[hours]
    once = hour_rows(coupling[0], hour[0], hours, 1)
    thrice = hour_rows(coupling[0], hour[0], hours, 3)
    sums = [jnp.zeros(right.shape[1:], F32) for _ in range(4)]
    for b in range(right.shape[0]):
        start = right[b]
        image = mix(once, first, b)
        sums[0] += start * start
        sums[1] += start * image
        sums[2] += image * image
        sums[3] += mix(thrice, first, b) * second[b]
    rows = [jnp.sum(s, axis=0, keepdims=True) for s in sums]
    out[...] = jnp.concatenate(rows + rows, axis=0)


def finish_body(hours, parts, coupling, hour, right, *refs):
    sums, refs = refs[:parts], refs[parts:]
    first, second, (solution, residual) = refs[:hours], refs[hours:-2], refs[-2:]
    once = hour_rows(coupling[0], hour[0], hours, 1)
    twice = hour_rows(coupling[0], hour[0], hours, 2)
    moment = functools.reduce(jnp.add, [s[...] for s in sums])
    m0, m1, m2, m3 = (moment[k : k + 1] for k in range(4))
    alpha = m0 / m1
    norm = alpha * alpha * m2 - m0
    lift = 1.0 + norm / m0
    step = norm / (lift * lift * m1 - 2.0 * lift * alpha * m2 + alpha * alpha * m3)
    on_right = alpha + step * lift
    on_first = step * alpha
    for b in range(right.shape[0]):
        start = right[b]
        image = mix(once, first, b)
        solution[b] = on_right * start - on_first * image
        residual[b] = start - on_right * image + on_first * mix(twice, second, b)


def shards(
    right_side,
    kappa_sq,
    time_coupling,
    near_stiffness,
    far_stiffness,
    near_columns,
    face_blocks,
    face_counts,
):
    right = right_side.reshape(right_side.shape[1:])
    hours = lax.axis_size("tm")
    hour = lax.axis_index("tm").reshape(1)
    headings, slots = face_blocks.shape[1:]
    stride = lax.axis_size(SPACE) // 4 + 1
    offsets = (1, -1, 2, -2, stride, -stride)
    faces = jnp.swapaxes(face_blocks, 1, 2)
    columns = jnp.swapaxes(near_columns, 0, 1)
    face = struct(slots, *right.shape[1:])
    outgoing = call(pack_body, [face] * headings, [smem(), vmem()], faces, right)

    def far(start, arrived, pack):
        body = functools.partial(far_body, headings, slots, pack)
        outs = [struct(*right.shape)] + [face] * (headings if pack else 0)
        ins = [smem(), smem()] + [vmem()] * (2 + headings)
        return call(body, outs, ins, faces, face_counts, far_stiffness, start, *arrived)

    arrived = exchange(outgoing, offsets)
    start = near(columns, kappa_sq, near_stiffness, right)
    first, *outgoing = far(start, arrived, True)
    arrived = exchange(outgoing, offsets)
    first_hours = [first, *rotations(first, "tm")]
    start = near(columns, kappa_sq, near_stiffness, first)
    (second,) = far(start, arrived, False)
    second_hours = [second, *rotations(second, "tm")]

    moments = call(
        functools.partial(moments_body, hours),
        struct(8, right.shape[2]),
        [smem(), smem()] + [vmem()] * (2 + hours),
        time_coupling,
        hour,
        right,
        second,
        *first_hours,
    )
    moments = total_over(moments, ("tm", "rep"))
    if lax.axis_size("mesh") > 4:
        sums = [lax.psum(moments, "mesh")]
    else:
        sums = [moments, *rotations(moments, "mesh")]
    solution_field, residual = call(
        functools.partial(finish_body, hours, len(sums)),
        [struct(*right.shape)] * 2,
        [smem(), smem()] + [vmem()] * (1 + len(sums) + 2 * hours),
        time_coupling,
        hour,
        right,
        *sums,
        *first_hours,
        *second_hours,
    )
    return (solution_field[None], residual[None])


def solution(mesh):
    placed = (
        P(("grp", "tm"), SPACE, None, None),
        P(("grp", "mesh", "rep"), None),
        P("grp"),
        P(SPACE, None, None),
        P(SPACE, None, None),
        P(SPACE, None),
        P(SPACE, None, None),
        P(SPACE, None),
    )
    return jax.shard_map(
        shards,
        mesh=mesh,
        in_specs=placed,
        out_specs=(
            P(("grp", "tm"), SPACE, None, None),
            P(("grp", "tm"), SPACE, None, None),
        ),
        check_vma=False,
    )
```

```python
import functools

import jax
import jax.numpy as jnp
from jax import lax
from jax.experimental import pallas as pl
from jax.experimental.pallas import tpu as pltpu
from jax.sharding import PartitionSpec as P

SPACE = ("mesh", "rep")
F32 = jnp.float32
BF16 = jnp.bfloat16
EARLY = (0, 2, 4)


def struct(*shape, dtype=F32):
    return jax.ShapeDtypeStruct(shape, dtype)


def call(body, outs, scalars, vectors, scratch=()):
    spaces = [pltpu.SMEM] * len(scalars) + [pltpu.VMEM] * len(vectors)
    return pl.pallas_call(
        body,
        out_shape=outs,
        in_specs=[pl.BlockSpec(memory_space=space) for space in spaces],
        out_specs=jax.tree.map(lambda _: pl.BlockSpec(memory_space=pltpu.VMEM), outs),
        scratch_shapes=scratch,
        compiler_params=pltpu.CompilerParams(vmem_limit_bytes=40 << 20),
    )(*scalars, *vectors)


def total(values):
    return functools.reduce(jnp.add, values)


def halves(value):
    high = value.astype(BF16)
    return high, (value - high.astype(F32)).astype(BF16)


def group_of(shape, hours):
    lanes = shape[-1]
    return lax.broadcasted_iota(jnp.int32, shape, len(shape) - 1) // (lanes // hours)


def turned(value, places, hours):
    width = value.shape[-1] // hours
    result = value
    for k in range(1, hours):
        result = jnp.where(places == k, pltpu.roll(value, k * width, value.ndim - 1), result)
    return result


def pack_lanes(hours, hour, field, outs):
    group = group_of(field.shape[1:], hours)
    for r, out in enumerate(outs):
        target = lax.rem(hour + r + 1, hours)
        for j in range(out.shape[0]):
            packed = None
            for i in range(hours):
                part = turned(field[j * hours + i], lax.rem(i - target + hours, hours), hours)
                packed = part if i == 0 else jnp.where(group == i, part, packed)
            out[j] = packed


def merge_lanes(hours, hour, own, packs, block):
    group = group_of(own.shape, hours)
    for r, pack in enumerate(packs):
        source = lax.rem(hour + hours - r - 1, hours)
        part = pack[block // hours]
        part = turned(part, lax.rem(source - block % hours + hours, hours), hours)
        own = jnp.where(group == source, part, own)
    return own


def couple(hours, coupling, value):
    lanes = value.shape[-1]
    width = lanes // hours
    before, after = (pltpu.roll(value, d, value.ndim - 1) for d in (width, lanes - width))
    if hours == 2:
        return value - coupling * before
    group = group_of(value.shape, hours)
    sides = jnp.where(group > 0, before, 0.0) + jnp.where(group < hours - 1, after, 0.0)
    return value - coupling * sides


def pack_faces(faces, field, headings, outs):
    for e, out in zip(headings, outs):
        for f in range(out.shape[0]):
            out[f] = field[faces[0, f, e]]


def far_product(stiffness, q, block):
    high, low = halves(block)
    right = jnp.concatenate([high, high, low], axis=0)
    return jnp.dot(stiffness[q], right, preferred_element_type=F32)


def landing(faces, counts, e, f, spare):
    return jnp.where(f < counts[0, e], faces[0, f, e], spare)


def open_body(hours, faces, hour, field, *outs):
    split = len(EARLY)
    pack_faces(faces, field, EARLY, outs[:split])
    pack_lanes(hours, hour[0], field, outs[split:])


def turn_body(hours, faces, hour, field, *refs):
    packs, out, faces_out = refs[: hours - 1], refs[hours - 1], refs[hours:]
    for b in range(field.shape[0]):
        out[b] = merge_lanes(hours, hour[0], field[b], packs, b)
    pack_faces(faces, out, [e ^ 1 for e in EARLY], faces_out)


def split_body(stiffness, out):
    width = stiffness.shape[1]
    for q in range(out.shape[0]):
        high, low = halves(stiffness[0, :, q * width : (q + 1) * width])
        out[q] = jnp.concatenate([high, low, high], axis=1)


def near_body(count, columns, kappa, stiffness, *refs):
    fields, outs, (high, low, diagonal) = refs[:count], refs[count:-3], refs[-3:]
    blocks = stiffness.shape[0]
    slots = columns.shape[0]
    lanes = fields[0].shape[2]
    diagonal[...] = jnp.transpose(kappa[...])
    for n, field in enumerate(fields):
        part = slice(n * lanes, (n + 1) * lanes)
        for b in range(blocks):
            high[b, :, part], low[b, :, part] = halves(field[b])
    for b in range(blocks):
        index = [columns[k, b] for k in range(slots)]
        highs = jnp.concatenate([high[i] for i in index], axis=0)
        lows = jnp.concatenate([low[i] for i in index], axis=0)
        left_high, left_low = halves(stiffness[b])
        near = jnp.dot(left_high, highs, preferred_element_type=F32)
        near += jnp.dot(left_low, highs, preferred_element_type=F32)
        near += jnp.dot(left_high, lows, preferred_element_type=F32)
        weight = 3.0 + diagonal[:, b : b + 1]
        for n, (field, out) in enumerate(zip(fields, outs)):
            out[b] = near[:, n * lanes : (n + 1) * lanes] + weight * field[b]


def near(columns, kappa, stiffness, fields):
    blocks, width, lanes = fields[0].shape
    return call(
        functools.partial(near_body, len(fields)),
        [struct(*field.shape) for field in fields],
        [columns],
        [kappa, stiffness, *fields],
        [
            pltpu.VMEM((blocks, width, lanes * len(fields)), BF16),
            pltpu.VMEM((blocks, width, lanes * len(fields)), BF16),
            pltpu.VMEM((width, blocks), F32),
        ],
    )


def early_products(stiffness, arrived, out):
    slots = arrived[0].shape[0]
    for n, e in enumerate(EARLY):
        for f in range(slots):
            out[n * slots + f] = far_product(stiffness, (e ^ 1) * slots + f, arrived[n][f])


def early_body(hours, hour, stiffness, *refs):
    count = len(EARLY)
    arrived, (out, *packs) = refs[:count], refs[count:]
    early_products(stiffness, arrived, out)
    pack_lanes(hours, hour[0], out, packs)


def gather_far(hours, faces, counts, hour, stiffness, own, packs, arrived, near_part, field):
    blocks = near_part.shape[0]
    slots = arrived[0].shape[0]
    for b in range(blocks):
        field[b] = near_part[b]
    for n, e in enumerate(EARLY):
        for f in range(slots):
            q = n * slots + f
            block = landing(faces, counts, e ^ 1, f, blocks)
            field[block] += merge_lanes(hours, hour[0], own[q], packs, q)
            block = landing(faces, counts, e, f, blocks)
            field[block] += far_product(stiffness, e * slots + f, arrived[n][f])


def middle_body(hours, faces, counts, hour, coupling, stiffness, near_part, own, *refs):
    count, turns = len(EARLY), hours - 1
    packs, arrived = refs[:turns], refs[turns : turns + count]
    first, image, *rest, field = refs[turns + count :]
    faces_out, image_packs, first_packs = (
        rest[:count],
        rest[count : count + turns],
        rest[count + turns :],
    )
    gather_far(hours, faces, counts, hour, stiffness, own, packs, arrived, near_part, field)
    for b in range(first.shape[0]):
        once = couple(hours, coupling[0], field[b])
        first[b] = once
        image[b] = couple(hours, coupling[0], once)
    pack_lanes(hours, hour[0], image, image_packs)
    pack_faces(faces, image, EARLY, faces_out)
    pack_lanes(hours, hour[0], first, first_packs)


def moments_body(hours, faces, counts, hour, right, first, second, own, out):
    slots = own.shape[0] // len(EARLY)
    sums = [jnp.zeros(right.shape[1:], F32) for _ in range(4)]
    for b in range(right.shape[0]):
        start, image = right[b], first[b]
        sums[0] += start * start
        sums[1] += start * image
        sums[2] += image * image
        sums[3] += image * second[b]
    for n, e in enumerate(EARLY):
        for f in range(slots):
            weight = jnp.where(f < counts[0, e ^ 1], 2.0, 0.0)
            sums[3] += weight * (first[faces[0, f, e ^ 1]] * own[n * slots + f])
    rows = jnp.concatenate([jnp.sum(s, axis=0, keepdims=True) for s in sums] * 2, axis=0)
    width = rows.shape[1] // hours
    rows = total([rows] + [pltpu.roll(rows, k * width, 1) for k in range(1, hours)])
    out[...] = jnp.where(group_of(rows.shape, hours) == hour[0], rows, 0.0)


def close_body(hours, parts, faces, counts, hour, stiffness, right, first, near_part, own, *refs):
    count, turns = len(EARLY), hours - 1
    sums, refs = refs[:parts], refs[parts:]
    first_packs, packs, arrived = refs[:turns], refs[turns : 2 * turns], refs[2 * turns :][:count]
    solution, residual, field = refs[2 * turns + count :]
    moment = total([s[...] for s in sums])
    m0, m1, m2, m3 = (moment[k : k + 1] for k in range(4))
    alpha = m0 / m1
    norm = alpha * alpha * m2 - m0
    lift = 1.0 + norm / m0
    step = norm / (lift * lift * m1 - 2.0 * lift * alpha * m2 + alpha * alpha * m3)
    on_right = alpha + step * lift
    on_first = step * alpha
    gather_far(hours, faces, counts, hour, stiffness, own, packs, arrived, near_part, field)
    for b in range(right.shape[0]):
        start = right[b]
        image = merge_lanes(hours, hour[0], first[b], first_packs, b)
        solution[b] = on_right * start - on_first * image
        residual[b] = start - on_right * image + on_first * field[b]


def shifted(value, axes, sizes, steps):
    route = []
    for source in range(functools.reduce(lambda a, b: a * b, sizes)):
        rest, target, scale = source, 0, 1
        for size, step in reversed(list(zip(sizes, steps))):
            rest, place = divmod(rest, size)
            target += (place + step) % size * scale
            scale *= size
        route.append((source, target))
    return lax.ppermute(value, axes, route)


def send_faces(outgoing, headings, offsets):
    count = lax.axis_size(SPACE)
    return [shifted(v, SPACE, (count,), (offsets[e],)) for v, e in zip(outgoing, headings)]


def send_lanes(packs):
    hours = lax.axis_size("tm")
    return [shifted(v, ("tm",), (hours,), (r + 1,)) for r, v in enumerate(packs)]


def everyone(value, axes):
    sizes = [lax.axis_size(axis) for axis in axes]
    size = functools.reduce(lambda a, b: a * b, sizes)
    if size > 4:
        return [lax.psum(value, axes)]
    steps = [[]]
    for n in sizes:
        steps = [s + [k] for s in steps for k in range(n)]
    return [value] + [shifted(value, axes, sizes, s) for s in steps[1:]]


def shards(
    right_side,
    kappa_sq,
    time_coupling,
    near_stiffness,
    far_stiffness,
    near_columns,
    face_blocks,
    face_counts,
):
    right = right_side.reshape(right_side.shape[1:])
    blocks, width, lanes = right.shape
    hours = lax.axis_size("tm")
    hour = lax.axis_index("tm").reshape(1)
    headings, slots = face_blocks.shape[1:]
    stride = lax.axis_size(SPACE) // 4 + 1
    offsets = (1, -1, 2, -2, stride, -stride)
    late = [e ^ 1 for e in EARLY]
    faces = jnp.swapaxes(face_blocks, 1, 2)
    columns = jnp.swapaxes(near_columns, 0, 1)
    counts = face_counts
    field = struct(*right.shape)
    face = [struct(slots, width, lanes)] * len(EARLY)
    pack = [struct(blocks // hours, width, lanes)] * (hours - 1)
    product = struct(len(EARLY) * slots, width, lanes)
    product_pack = [struct(product.shape[0] // hours, width, lanes)] * (hours - 1)
    spare = [pltpu.VMEM((blocks + 1, width, lanes), F32)]

    def body(function, *sizes):
        return functools.partial(function, hours, *sizes)

    def unpack(values, *sizes):
        values, result = list(values), []
        for n in sizes:
            result.append(values[:n])
            values = values[n:]
        return result

    outs = call(body(open_body), face + pack, [faces, hour], [right])
    outgoing, packs = unpack(outs, len(face), len(pack))
    packs = send_lanes(packs)
    early = send_faces(outgoing, EARLY, offsets)
    probe_right, *outgoing = call(
        body(turn_body), [field] + face, [faces, hour], [right, *packs]
    )
    arrived = send_faces(outgoing, late, offsets)
    stiffness = call(
        split_body, struct(headings * slots, width, 3 * width, dtype=BF16), [], [far_stiffness]
    )
    (near_part,) = near(columns, kappa_sq, near_stiffness, [probe_right])
    own, *packs = call(
        body(early_body), [product] + product_pack, [hour], [stiffness, *early]
    )
    packs = send_lanes(packs)
    outs = call(
        body(middle_body),
        [field, field] + face + pack + pack,
        [faces, counts, hour, time_coupling],
        [stiffness, near_part, own, *packs, *arrived],
        spare,
    )
    (first, image), outgoing, packs, first_packs = unpack(
        outs, 2, len(face), len(pack), len(pack)
    )

    packs = send_lanes(packs)
    early = send_faces(outgoing, EARLY, offsets)
    hour_image, *outgoing = call(body(turn_body), [field] + face, [faces, hour], [image, *packs])
    arrived = send_faces(outgoing, late, offsets)
    first_packs = send_lanes(first_packs)
    near_probe, near_hour = near(columns, kappa_sq, near_stiffness, [image, hour_image])
    own, *packs = call(
        body(early_body), [product] + product_pack, [hour], [stiffness, *early]
    )
    sums = call(
        body(moments_body),
        struct(8, lanes),
        [faces, counts, hour],
        [probe_right, first, near_probe, own],
    )
    sums = everyone(total(everyone(sums, ("tm", "rep"))), ("mesh",))
    packs = send_lanes(packs)
    solution_field, residual = call(
        body(close_body, len(sums)),
        [field, field],
        [faces, counts, hour],
        [stiffness, right, first, near_hour, own, *sums, *first_packs, *packs, *arrived],
        spare,
    )
    return (solution_field[None], residual[None])


def solution(mesh):
    placed = (
        P(("grp", "tm"), SPACE, None, None),
        P(("grp", "mesh", "rep"), None),
        P("grp"),
        P(SPACE, None, None),
        P(SPACE, None, None),
        P(SPACE, None),
        P(SPACE, None, None),
        P(SPACE, None),
    )
    return jax.shard_map(
        shards,
        mesh=mesh,
        in_specs=placed,
        out_specs=(
            P(("grp", "tm"), SPACE, None, None),
            P(("grp", "tm"), SPACE, None, None),
        ),
        check_vma=False,
    )
```

```python
import functools

import jax
import jax.numpy as jnp
from jax import lax
from jax.experimental import pallas as pl
from jax.experimental.pallas import tpu as pltpu
from jax.sharding import PartitionSpec as P

SPACE = ("mesh", "rep")
F32 = jnp.float32
BF16 = jnp.bfloat16
PLUS = 3


def struct(*shape, dtype=F32):
    return jax.ShapeDtypeStruct(shape, dtype)


def call(body, outs, scalars, vectors, scratch=()):
    spaces = [pltpu.SMEM] * len(scalars) + [pltpu.VMEM] * len(vectors)
    return pl.pallas_call(
        body,
        out_shape=outs,
        in_specs=[pl.BlockSpec(memory_space=space) for space in spaces],
        out_specs=jax.tree.map(lambda _: pl.BlockSpec(memory_space=pltpu.VMEM), outs),
        scratch_shapes=scratch,
        compiler_params=pltpu.CompilerParams(vmem_limit_bytes=40 << 20),
    )(*scalars, *vectors)


def total(values):
    return functools.reduce(jnp.add, values)


def halves(value):
    high = value.astype(BF16)
    return high, (value - high.astype(F32)).astype(BF16)


def group_of(shape, hours):
    lanes = shape[-1]
    return lax.broadcasted_iota(jnp.int32, shape, len(shape) - 1) // (lanes // hours)


def turned(value, places, hours):
    width = value.shape[-1] // hours
    result = value
    for k in range(1, hours):
        result = jnp.where(places == k, pltpu.roll(value, k * width, value.ndim - 1), result)
    return result


def pack_lanes(hours, hour, field, outs):
    group = group_of(field.shape[1:], hours)
    for r, out in enumerate(outs):
        target = lax.rem(hour + r + 1, hours)
        for j in range(out.shape[0]):
            packed = None
            for i in range(hours):
                part = turned(field[j * hours + i], lax.rem(i - target + hours, hours), hours)
                packed = part if i == 0 else jnp.where(group == i, part, packed)
            out[j] = packed


def merge_lanes(hours, hour, own, packs, block):
    group = group_of(own.shape, hours)
    for r, pack in enumerate(packs):
        source = lax.rem(hour + hours - r - 1, hours)
        part = pack[block // hours]
        part = turned(part, lax.rem(source - block % hours + hours, hours), hours)
        own = jnp.where(group == source, part, own)
    return own


def couple(hours, coupling, value):
    lanes = value.shape[-1]
    width = lanes // hours
    before, after = (pltpu.roll(value, d, value.ndim - 1) for d in (width, lanes - width))
    if hours == 2:
        return value - coupling * before
    group = group_of(value.shape, hours)
    sides = jnp.where(group > 0, before, 0.0) + jnp.where(group < hours - 1, after, 0.0)
    return value - coupling * sides


def pack_faces(faces, field, headings, outs):
    slots = faces.shape[1]
    places = [out.at[k] for out in outs for k in range(out.shape[0])]
    for m, place in enumerate(places):
        place[...] = field[faces[0, m % slots, headings[m // slots]]]


def far_product(stiffness, q, block):
    high, low = halves(block)
    right = jnp.concatenate([high, high, low], axis=0)
    return jnp.dot(stiffness[q], right, preferred_element_type=F32)


def landing(faces, counts, e, f, spare):
    return jnp.where(f < counts[0, e], faces[0, f, e], spare)


def open_body(hours, faces, plan, hour, field, *outs):
    pack_lanes(hours, hour[0], field, outs[: hours - 1])
    pack_faces(faces, field, [plan[n] for n in range(PLUS)], outs[hours - 1 :])


def turn_body(hours, extra, faces, plan, hour, field, _, *refs):
    packs, refs = refs[: hours - 1], refs[hours - 1 :]
    (out, *faces_out), others = refs[extra:], []
    if extra:
        others, faces_out = faces_out[: hours - 1], faces_out[hours - 1 :]
    for b in range(field.shape[0]):
        out[b] = merge_lanes(hours, hour[0], field[b], packs, b)
    pack_faces(faces, out, [plan[PLUS + n] ^ 1 for n in range(PLUS)], faces_out)
    if extra:
        pack_lanes(hours, hour[0], refs[0], others)


def split_body(stiffness, out):
    width = stiffness.shape[1]
    for q in range(out.shape[0]):
        high, low = halves(stiffness[0, :, q * width : (q + 1) * width])
        out[q] = jnp.concatenate([high, low, high], axis=1)


def near_body(count, columns, kappa, stiffness, *refs):
    fields, outs, (high, low, diagonal) = refs[:count], refs[count:-3], refs[-3:]
    blocks = stiffness.shape[0]
    slots = columns.shape[0]
    lanes = fields[0].shape[2]
    diagonal[...] = jnp.transpose(kappa[...])
    for n, field in enumerate(fields):
        part = slice(n * lanes, (n + 1) * lanes)
        for b in range(blocks):
            high[b, :, part], low[b, :, part] = halves(field[b])
    for b in range(blocks):
        index = [columns[k, b] for k in range(slots)]
        highs = jnp.concatenate([high[i] for i in index], axis=0)
        lows = jnp.concatenate([low[i] for i in index], axis=0)
        left_high, left_low = halves(stiffness[b])
        near = jnp.dot(left_high, highs, preferred_element_type=F32)
        near += jnp.dot(left_low, highs, preferred_element_type=F32)
        near += jnp.dot(left_high, lows, preferred_element_type=F32)
        weight = 3.0 + diagonal[:, b : b + 1]
        for n, (field, out) in enumerate(zip(fields, outs)):
            out[b] = near[:, n * lanes : (n + 1) * lanes] + weight * field[b]


def near(columns, kappa, stiffness, fields):
    blocks, width, lanes = fields[0].shape
    return call(
        functools.partial(near_body, len(fields)),
        [struct(*field.shape) for field in fields],
        [columns],
        [kappa, stiffness, *fields],
        [
            pltpu.VMEM((blocks, width, lanes * len(fields)), BF16),
            pltpu.VMEM((blocks, width, lanes * len(fields)), BF16),
            pltpu.VMEM((width, blocks), F32),
        ],
    )


def early_body(hours, plan, hour, stiffness, *refs):
    arrived, (out, *packs) = refs[:PLUS], refs[PLUS + 2 :]
    slots = out.shape[0] // PLUS
    for n in range(PLUS):
        for f in range(slots):
            q = (plan[PLUS + n] ^ 1) * slots + f
            out[n * slots + f] = far_product(stiffness, q, arrived[n][f])
    pack_lanes(hours, hour[0], out, packs)


def gather_far(hours, faces, counts, plan, hour, stiffness, own, packs, arrived, near_part, field):
    blocks = near_part.shape[0]
    slots = own.shape[0] // PLUS
    for b in range(blocks):
        field[b] = near_part[b]
    for n in range(PLUS):
        e = plan[n]
        for f in range(slots):
            q = n * slots + f
            block = landing(faces, counts, plan[PLUS + n] ^ 1, f, blocks)
            field[block] += merge_lanes(hours, hour[0], own[q], packs, q)
            block = landing(faces, counts, e, f, blocks)
            field[block] += far_product(stiffness, e * slots + f, arrived[n][f])


def middle_body(hours, faces, counts, plan, hour, coupling, stiffness, near_part, own, *refs):
    turns = hours - 1
    packs, arrived = refs[:turns], refs[turns : turns + PLUS]
    first, image, *rest, field = refs[turns + PLUS :]
    image_packs, faces_out = rest[:turns], rest[turns:]
    gather_far(hours, faces, counts, plan, hour, stiffness, own, packs, arrived, near_part, field)
    for b in range(first.shape[0]):
        once = couple(hours, coupling[0], field[b])
        first[b] = once
        image[b] = couple(hours, coupling[0], once)
    pack_lanes(hours, hour[0], image, image_packs)
    pack_faces(faces, image, [plan[n] for n in range(PLUS)], faces_out)


def moments_body(hours, faces, counts, plan, hour, right, first, second, own, out):
    slots = own.shape[0] // PLUS
    sums = [jnp.zeros(right.shape[1:], F32) for _ in range(4)]
    for b in range(right.shape[0]):
        start, image = right[b], first[b]
        sums[0] += start * start
        sums[1] += start * image
        sums[2] += image * image
        sums[3] += image * second[b]
    for n in range(PLUS):
        e = plan[PLUS + n] ^ 1
        for f in range(slots):
            weight = jnp.where(f < counts[0, e], 2.0, 0.0)
            sums[3] += weight * (first[faces[0, f, e]] * own[n * slots + f])
    rows = jnp.concatenate([jnp.sum(s, axis=0, keepdims=True) for s in sums] * 2, axis=0)
    width = rows.shape[1] // hours
    rows = total([rows] + [pltpu.roll(rows, k * width, 1) for k in range(1, hours)])
    out[...] = jnp.where(group_of(rows.shape, hours) == hour[0], rows, 0.0)


def close_body(
    hours, parts, faces, counts, plan, hour, stiffness, right, first, near_part, own, *refs
):
    turns = hours - 1
    sums, refs = refs[:parts], refs[parts:]
    first_packs, packs, arrived = refs[:turns], refs[turns : 2 * turns], refs[2 * turns :][:PLUS]
    solution, residual, field = refs[2 * turns + PLUS :]
    moment = total([s[...] for s in sums])
    m0, m1, m2, m3 = (moment[k : k + 1] for k in range(4))
    alpha = m0 / m1
    norm = alpha * alpha * m2 - m0
    lift = 1.0 + norm / m0
    step = norm / (lift * lift * m1 - 2.0 * lift * alpha * m2 + alpha * alpha * m3)
    on_right = alpha + step * lift
    on_first = step * alpha
    gather_far(hours, faces, counts, plan, hour, stiffness, own, packs, arrived, near_part, field)
    for b in range(right.shape[0]):
        start = right[b]
        image = merge_lanes(hours, hour[0], first[b], first_packs, b)
        solution[b] = on_right * start - on_first * image
        residual[b] = start - on_right * image + on_first * field[b]


def shifted(value, axes, sizes, steps):
    route = []
    for source in range(functools.reduce(lambda a, b: a * b, sizes)):
        rest, target, scale = source, 0, 1
        for size, step in reversed(list(zip(sizes, steps))):
            rest, place = divmod(rest, size)
            target += (place + step) % size * scale
            scale *= size
        route.append((source, target))
    return lax.ppermute(value, axes, route)


def paired(stride):
    return stride == 3 and lax.axis_size("rep") == 2


def face_plan(stride):
    if not paired(stride):
        return jnp.array([2, 0, 4, 2, 0, 4], jnp.int32)
    odd = lax.axis_index("rep") == 1
    near, long = jnp.where(odd, 0, 4), jnp.where(odd, 4, 0)
    two = jnp.int32(2)
    return jnp.stack([two, near, long, two, long, near]).astype(jnp.int32)


def send_faces(outgoing, stride, sign):
    mesh, rep = (lax.axis_size(axis) for axis in SPACE)
    count = mesh * rep
    if not paired(stride):
        return [
            shifted(v, SPACE, (count,), (sign * d,)) for v, d in zip(outgoing, (2, 1, stride))
        ]
    both, single = outgoing
    slots = both.shape[0] // 2
    hop = (1, 3) if sign > 0 else (-3, -1)
    both = shifted(both, ("mesh",), (mesh,), (sign,))
    single = lax.ppermute(single, SPACE, [(i, (i + hop[i % 2]) % count) for i in range(count)])
    relayed = shifted(both[slots:], ("rep",), (rep,), (1,))
    return [both, relayed, single]


def send_lanes(packs):
    hours = lax.axis_size("tm")
    return [shifted(v, ("tm",), (hours,), (r + 1,)) for r, v in enumerate(packs)]


def everyone(value, axes):
    sizes = [lax.axis_size(axis) for axis in axes]
    size = functools.reduce(lambda a, b: a * b, sizes)
    if size > 4:
        return [lax.psum(value, axes)]
    steps = [[]]
    for n in sizes:
        steps = [s + [k] for s in steps for k in range(n)]
    return [value] + [shifted(value, axes, sizes, s) for s in steps[1:]]


def shards(
    right_side,
    kappa_sq,
    time_coupling,
    near_stiffness,
    far_stiffness,
    near_columns,
    face_blocks,
    face_counts,
):
    right = right_side.reshape(right_side.shape[1:])
    blocks, width, lanes = right.shape
    hours = lax.axis_size("tm")
    hour = lax.axis_index("tm").reshape(1)
    headings, slots = face_blocks.shape[1:]
    stride = lax.axis_size(SPACE) // 4 + 1
    faces = jnp.swapaxes(face_blocks, 1, 2)
    columns = jnp.swapaxes(near_columns, 0, 1)
    counts = face_counts
    plan = face_plan(stride)
    field = struct(*right.shape)
    sent = [2 * slots, slots] if paired(stride) else [slots] * PLUS
    face = [struct(n, width, lanes) for n in sent]
    pack = [struct(blocks // hours, width, lanes)] * (hours - 1)
    product = struct(PLUS * slots, width, lanes)
    product_pack = [struct(product.shape[0] // hours, width, lanes)] * (hours - 1)
    spare = [pltpu.VMEM((blocks + 1, width, lanes), F32)]
    turns = hours - 1

    def body(function, *sizes):
        return functools.partial(function, hours, *sizes)

    def early_products(early, after):
        own, *packs = call(
            body(early_body), [product] + product_pack, [plan, hour], [stiffness, *early, *after]
        )
        return own, packs

    outs = call(body(open_body), pack + face, [faces, plan, hour], [right])
    packs = send_lanes(outs[:turns])
    early = send_faces(outs[turns:], stride, 1)
    probe_right, *outgoing = call(
        body(turn_body, 0), [field] + face, [faces, plan, hour], [right, early[-1], *packs]
    )
    arrived = send_faces(outgoing, stride, -1)
    stiffness = call(
        split_body, struct(headings * slots, width, 3 * width, dtype=BF16), [], [far_stiffness]
    )
    (near_part,) = near(columns, kappa_sq, near_stiffness, [probe_right])
    own, packs = early_products(early, [near_part, arrived[-1]])
    packs = send_lanes(packs)
    first, image, *outs = call(
        body(middle_body),
        [field, field] + pack + face,
        [faces, counts, plan, hour, time_coupling],
        [stiffness, near_part, own, *packs, *arrived],
        spare,
    )

    packs = send_lanes(outs[:turns])
    early = send_faces(outs[turns:], stride, 1)
    hour_image, *outs = call(
        body(turn_body, 1), [field] + pack + face, [faces, plan, hour], [image, early[-1], *packs, first]
    )
    first_packs = send_lanes(outs[:turns])
    arrived = send_faces(outs[turns:], stride, -1)
    near_probe, near_hour = near(columns, kappa_sq, near_stiffness, [image, hour_image])
    own, packs = early_products(early, [near_hour, arrived[-1]])
    sums = call(
        body(moments_body),
        struct(8, lanes),
        [faces, counts, plan, hour],
        [probe_right, first, near_probe, own],
    )
    sums = everyone(total(everyone(sums, ("tm", "rep"))), ("mesh",))
    packs = send_lanes(packs)
    solution_field, residual = call(
        body(close_body, len(sums)),
        [field, field],
        [faces, counts, plan, hour],
        [stiffness, right, first, near_hour, own, *sums, *first_packs, *packs, *arrived],
        spare,
    )
    return (solution_field[None], residual[None])


def solution(mesh):
    placed = (
        P(("grp", "tm"), SPACE, None, None),
        P(("grp", "mesh", "rep"), None),
        P("grp"),
        P(SPACE, None, None),
        P(SPACE, None, None),
        P(SPACE, None),
        P(SPACE, None, None),
        P(SPACE, None),
    )
    return jax.shard_map(
        shards,
        mesh=mesh,
        in_specs=placed,
        out_specs=(
            P(("grp", "tm"), SPACE, None, None),
            P(("grp", "tm"), SPACE, None, None),
        ),
        check_vma=False,
    )
```

```python
import functools

import jax
import jax.numpy as jnp
from jax import lax
from jax.experimental import pallas as pl
from jax.experimental.pallas import tpu as pltpu
from jax.sharding import PartitionSpec as P

SPACE = ("mesh", "rep")
F32 = jnp.float32
BF16 = jnp.bfloat16
EARLY = (4, 2, 0)
PLUS = len(EARLY)
ORDER = (0, 40, 0, 160)


def struct(*shape, dtype=F32):
    return jax.ShapeDtypeStruct(shape, dtype)


def call(body, outs, scalars, vectors, scratch=(), weight=0):
    spaces = [pltpu.SMEM] * len(scalars) + [pltpu.VMEM] * len(vectors)
    return pl.pallas_call(
        body,
        out_shape=outs,
        in_specs=[pl.BlockSpec(memory_space=space) for space in spaces],
        out_specs=jax.tree.map(lambda _: pl.BlockSpec(memory_space=pltpu.VMEM), outs),
        scratch_shapes=scratch,
        cost_estimate=pl.CostEstimate(
            flops=(weight << 30) + 1024, transcendentals=0, bytes_accessed=1024
        ),
        compiler_params=pltpu.CompilerParams(vmem_limit_bytes=40 << 20),
    )(*scalars, *vectors)


def total(values):
    return functools.reduce(jnp.add, values)


def halves(value):
    high = value.astype(BF16)
    return high, (value - high.astype(F32)).astype(BF16)


def group_of(shape, hours):
    lanes = shape[-1]
    return lax.broadcasted_iota(jnp.int32, shape, len(shape) - 1) // (lanes // hours)


def turned(value, places, hours):
    width = value.shape[-1] // hours
    result = value
    for k in range(1, hours):
        result = jnp.where(places == k, pltpu.roll(value, k * width, value.ndim - 1), result)
    return result


def pack_lanes(hours, hour, field, outs):
    group = group_of(field.shape[1:], hours)
    for r, out in enumerate(outs):
        target = lax.rem(hour + r + 1, hours)
        for j in range(out.shape[0]):
            packed = None
            for i in range(hours):
                part = turned(field[j * hours + i], lax.rem(i - target + hours, hours), hours)
                packed = part if i == 0 else jnp.where(group == i, part, packed)
            out[j] = packed


def merge_lanes(hours, hour, own, packs, block):
    group = group_of(own.shape, hours)
    for r, pack in enumerate(packs):
        source = lax.rem(hour + hours - r - 1, hours)
        part = pack[block // hours]
        part = turned(part, lax.rem(source - block % hours + hours, hours), hours)
        own = jnp.where(group == source, part, own)
    return own


def couple(hours, coupling, value):
    lanes = value.shape[-1]
    width = lanes // hours
    before, after = (pltpu.roll(value, d, value.ndim - 1) for d in (width, lanes - width))
    if hours == 2:
        return value - coupling * before
    group = group_of(value.shape, hours)
    sides = jnp.where(group > 0, before, 0.0) + jnp.where(group < hours - 1, after, 0.0)
    return value - coupling * sides


def pack_faces(faces, field, headings, outs):
    slots = faces.shape[1]
    places = [out.at[k] for out in outs for k in range(out.shape[0])]
    for m, place in enumerate(places):
        place[...] = field[faces[0, m % slots, headings[m // slots]]]


def far_product(stiffness, q, block):
    high, low = halves(block)
    right = jnp.concatenate([high, high, low], axis=0)
    return jnp.dot(stiffness[q], right, preferred_element_type=F32)


def landing(faces, counts, e, f, spare):
    return jnp.where(f < counts[0, e], faces[0, f, e], spare)


def open_body(hours, faces, hour, field, *outs):
    pack_lanes(hours, hour[0], field, outs[: hours - 1])
    pack_faces(faces, field, EARLY, outs[hours - 1 :])


def turn_body(hours, extra, faces, hour, field, *refs):
    packs, refs = refs[: hours - 1], refs[hours - 1 :]
    (out, *faces_out), others = refs[extra:], []
    if extra:
        others, faces_out = faces_out[: hours - 1], faces_out[hours - 1 :]
    for b in range(field.shape[0]):
        out[b] = merge_lanes(hours, hour[0], field[b], packs, b)
    pack_faces(faces, out, [e ^ 1 for e in EARLY], faces_out)
    if extra:
        pack_lanes(hours, hour[0], refs[0], others)


def split_body(stiffness, out):
    width = stiffness.shape[1]
    for q in range(out.shape[0]):
        high, low = halves(stiffness[0, :, q * width : (q + 1) * width])
        out[q] = jnp.concatenate([high, low, high], axis=1)


def near_body(count, columns, kappa, stiffness, *refs):
    fields, outs, (high, low, diagonal) = refs[:count], refs[count:-3], refs[-3:]
    blocks = stiffness.shape[0]
    slots = columns.shape[0]
    lanes = fields[0].shape[2]
    diagonal[...] = jnp.transpose(kappa[...])
    for n, field in enumerate(fields):
        part = slice(n * lanes, (n + 1) * lanes)
        for b in range(blocks):
            high[b, :, part], low[b, :, part] = halves(field[b])
    for b in range(blocks):
        index = [columns[k, b] for k in range(slots)]
        highs = jnp.concatenate([high[i] for i in index], axis=0)
        lows = jnp.concatenate([low[i] for i in index], axis=0)
        left_high, left_low = halves(stiffness[b])
        near = jnp.dot(left_high, highs, preferred_element_type=F32)
        near += jnp.dot(left_low, highs, preferred_element_type=F32)
        near += jnp.dot(left_high, lows, preferred_element_type=F32)
        weight = 3.0 + diagonal[:, b : b + 1]
        for n, (field, out) in enumerate(zip(fields, outs)):
            out[b] = near[:, n * lanes : (n + 1) * lanes] + weight * field[b]


def near(columns, kappa, stiffness, fields):
    blocks, width, lanes = fields[0].shape
    return call(
        functools.partial(near_body, len(fields)),
        [struct(*field.shape) for field in fields],
        [columns],
        [kappa, stiffness, *fields],
        [
            pltpu.VMEM((blocks, width, lanes * len(fields)), BF16),
            pltpu.VMEM((blocks, width, lanes * len(fields)), BF16),
            pltpu.VMEM((width, blocks), F32),
        ],
    )


def early_body(hours, hour, stiffness, *refs):
    arrived, (out, *packs) = refs[:PLUS], refs[PLUS:]
    slots = out.shape[0] // PLUS
    for n in range(PLUS):
        for f in range(slots):
            q = (EARLY[n] ^ 1) * slots + f
            out[n * slots + f] = far_product(stiffness, q, arrived[n][f])
    pack_lanes(hours, hour[0], out, packs)


def late_body(stiffness, *refs):
    arrived, out = refs[:PLUS], refs[-1]
    slots = out.shape[0] // PLUS
    for n in range(PLUS):
        for f in range(slots):
            out[n * slots + f] = far_product(stiffness, EARLY[n] * slots + f, arrived[n][f])


def gather_far(hours, faces, counts, hour, own, packs, late, near_part, field):
    blocks = near_part.shape[0]
    slots = own.shape[0] // PLUS
    for b in range(blocks):
        field[b] = near_part[b]
    for n in range(PLUS):
        e = EARLY[n]
        for f in range(slots):
            q = n * slots + f
            block = landing(faces, counts, e ^ 1, f, blocks)
            field[block] += merge_lanes(hours, hour[0], own[q], packs, q)
            block = landing(faces, counts, e, f, blocks)
            field[block] += late[q]


def middle_body(hours, faces, counts, hour, coupling, near_part, own, late, *refs):
    turns = hours - 1
    packs = refs[:turns]
    first, image, *rest, field = refs[turns:]
    image_packs, faces_out = rest[:turns], rest[turns:]
    gather_far(hours, faces, counts, hour, own, packs, late, near_part, field)
    for b in range(first.shape[0]):
        once = couple(hours, coupling[0], field[b])
        first[b] = once
        image[b] = couple(hours, coupling[0], once)
    pack_lanes(hours, hour[0], image, image_packs)
    pack_faces(faces, image, EARLY, faces_out)


def moments_body(hours, faces, counts, hour, right, first, second, own, out):
    slots = own.shape[0] // PLUS
    sums = [jnp.zeros(right.shape[1:], F32) for _ in range(4)]
    for b in range(right.shape[0]):
        start, image = right[b], first[b]
        sums[0] += start * start
        sums[1] += start * image
        sums[2] += image * image
        sums[3] += image * second[b]
    for n in range(PLUS):
        e = EARLY[n] ^ 1
        for f in range(slots):
            weight = jnp.where(f < counts[0, e], 2.0, 0.0)
            sums[3] += weight * (first[faces[0, f, e]] * own[n * slots + f])
    rows = jnp.concatenate([jnp.sum(s, axis=0, keepdims=True) for s in sums] * 2, axis=0)
    width = rows.shape[1] // hours
    rows = total([rows] + [pltpu.roll(rows, k * width, 1) for k in range(1, hours)])
    out[...] = jnp.where(group_of(rows.shape, hours) == hour[0], rows, 0.0)


def close_body(
    hours, parts, faces, counts, hour, right, first, near_part, own, late, *refs
):
    turns = hours - 1
    sums, refs = refs[:parts], refs[parts:]
    first_packs, packs = refs[:turns], refs[turns : 2 * turns]
    solution, residual, field = refs[2 * turns :]
    moment = total([s[...] for s in sums])
    m0, m1, m2, m3 = (moment[k : k + 1] for k in range(4))
    alpha = m0 / m1
    norm = alpha * alpha * m2 - m0
    lift = 1.0 + norm / m0
    step = norm / (lift * lift * m1 - 2.0 * lift * alpha * m2 + alpha * alpha * m3)
    on_right = alpha + step * lift
    on_first = step * alpha
    gather_far(hours, faces, counts, hour, own, packs, late, near_part, field)
    for b in range(right.shape[0]):
        start = right[b]
        image = merge_lanes(hours, hour[0], first[b], first_packs, b)
        solution[b] = on_right * start - on_first * image
        residual[b] = start - on_right * image + on_first * field[b]


def shifted(value, axes, sizes, steps):
    route = []
    for source in range(functools.reduce(lambda a, b: a * b, sizes)):
        rest, target, scale = source, 0, 1
        for size, step in reversed(list(zip(sizes, steps))):
            rest, place = divmod(rest, size)
            target += (place + step) % size * scale
            scale *= size
        route.append((source, target))
    return lax.ppermute(value, axes, route)


def send_faces(outgoing, offsets, opposite):
    count = lax.axis_size(SPACE)
    steps = [offsets[e ^ opposite] for e in EARLY]
    return [shifted(v, SPACE, (count,), (d,)) for v, d in zip(outgoing, steps)]


def send_lanes(packs):
    hours = lax.axis_size("tm")
    return [shifted(v, ("tm",), (hours,), (r + 1,)) for r, v in enumerate(packs)]


def everyone(value, axes):
    sizes = [lax.axis_size(axis) for axis in axes]
    size = functools.reduce(lambda a, b: a * b, sizes)
    if size > 4:
        return [lax.psum(value, axes)]
    steps = [[]]
    for n in sizes:
        steps = [s + [k] for s in steps for k in range(n)]
    return [value] + [shifted(value, axes, sizes, s) for s in steps[1:]]


def shards(
    right_side,
    kappa_sq,
    time_coupling,
    near_stiffness,
    far_stiffness,
    near_columns,
    face_blocks,
    face_counts,
):
    right = right_side.reshape(right_side.shape[1:])
    blocks, width, lanes = right.shape
    hours = lax.axis_size("tm")
    hour = lax.axis_index("tm").reshape(1)
    headings, slots = face_blocks.shape[1:]
    stride = lax.axis_size(SPACE) // 4 + 1
    faces = jnp.swapaxes(face_blocks, 1, 2)
    columns = jnp.swapaxes(near_columns, 0, 1)
    counts = face_counts
    offsets = (1, -1, 2, -2, stride, -stride)
    field = struct(*right.shape)
    face = [struct(slots, width, lanes)] * PLUS
    pack = [struct(blocks // hours, width, lanes)] * (hours - 1)
    product = struct(PLUS * slots, width, lanes)
    product_pack = [struct(product.shape[0] // hours, width, lanes)] * (hours - 1)
    spare = [pltpu.VMEM((blocks + 1, width, lanes), F32)]
    turns = hours - 1

    def body(function, *sizes):
        return functools.partial(function, hours, *sizes)

    def early_products(early, weight):
        own, *packs = call(
            body(early_body),
            [product] + product_pack,
            [hour],
            [stiffness, *early],
            weight=weight,
        )
        return own, packs

    def late_products(late, after, weight):
        return call(late_body, product, [], [stiffness, *late, *after], weight=weight)

    outs = call(body(open_body), pack + face, [faces, hour], [right])
    packs = send_lanes(outs[:turns])
    early = send_faces(outs[turns:], offsets, 0)
    probe_right, *outgoing = call(
        body(turn_body, 0), [field] + face, [faces, hour], [right, *packs]
    )
    arrived = send_faces(outgoing, offsets, 1)
    stiffness = call(
        split_body, struct(headings * slots, width, 3 * width, dtype=BF16), [], [far_stiffness]
    )
    (near_part,) = near(columns, kappa_sq, near_stiffness, [probe_right])
    own, packs = early_products(early, ORDER[0])
    packs = send_lanes(packs)
    late = late_products(arrived, [], ORDER[1])
    first, image, *outs = call(
        body(middle_body),
        [field, field] + pack + face,
        [faces, counts, hour, time_coupling],
        [near_part, own, late, *packs],
        spare,
    )

    packs = send_lanes(outs[:turns])
    early = send_faces(outs[turns:], offsets, 0)
    hour_image, *outs = call(
        body(turn_body, 1), [field] + pack + face, [faces, hour], [image, *packs, first]
    )
    first_packs = send_lanes(outs[:turns])
    arrived = send_faces(outs[turns:], offsets, 1)
    near_probe, near_hour = near(columns, kappa_sq, near_stiffness, [image, hour_image])
    own, packs = early_products(early, ORDER[2])
    sums = call(
        body(moments_body),
        struct(8, lanes),
        [faces, counts, hour],
        [probe_right, first, near_probe, own],
    )
    for axis in ("rep", "tm"):
        sums = total(everyone(sums, (axis,)))
    sums = everyone(sums, ("mesh",))
    packs = send_lanes(packs)
    late = late_products(arrived, first_packs, ORDER[3])
    solution_field, residual = call(
        body(close_body, len(sums)),
        [field, field],
        [faces, counts, hour],
        [right, first, near_hour, own, late, *sums, *first_packs, *packs],
        spare,
    )
    return (solution_field[None], residual[None])


def solution(mesh):
    placed = (
        P(("grp", "tm"), SPACE, None, None),
        P(("grp", "mesh", "rep"), None),
        P("grp"),
        P(SPACE, None, None),
        P(SPACE, None, None),
        P(SPACE, None),
        P(SPACE, None, None),
        P(SPACE, None),
    )
    return jax.shard_map(
        shards,
        mesh=mesh,
        in_specs=placed,
        out_specs=(
            P(("grp", "tm"), SPACE, None, None),
            P(("grp", "tm"), SPACE, None, None),
        ),
        check_vma=False,
    )
```

```python
import functools

import jax
import jax.numpy as jnp
from jax import lax
from jax.experimental import pallas as pl
from jax.experimental.pallas import tpu as pltpu
from jax.sharding import PartitionSpec as P

SPACE = ("mesh", "rep")
F32 = jnp.float32
BF16 = jnp.bfloat16
PHASES = (((4, 2), (5, 3, 0, 1)), ((4, 2, 0), (5, 3, 1)))
STAGES = (("rep", (1,)), ("tm", (1,)), ("mesh", (1, 2, 3)))
SPLIT = 2
PIECES = 4
ORDER = (40, 160, 0, 0)


def struct(*shape, dtype=F32):
    return jax.ShapeDtypeStruct(shape, dtype)


def call(body, outs, scalars, vectors, scratch=(), weight=0, outs_in=pltpu.VMEM):
    spaces = [pltpu.SMEM] * len(scalars) + [pltpu.VMEM] * len(vectors)
    return pl.pallas_call(
        body,
        out_shape=outs,
        in_specs=[pl.BlockSpec(memory_space=space) for space in spaces],
        out_specs=jax.tree.map(lambda _: pl.BlockSpec(memory_space=outs_in), outs),
        scratch_shapes=scratch,
        cost_estimate=pl.CostEstimate(
            flops=(weight << 30) + 1024, transcendentals=0, bytes_accessed=1024
        ),
        compiler_params=pltpu.CompilerParams(vmem_limit_bytes=40 << 20),
    )(*scalars, *vectors)


def total(values):
    return functools.reduce(jnp.add, values)


def halves(value):
    high = value.astype(BF16)
    return high, (value - high.astype(F32)).astype(BF16)


def group_of(shape, hours):
    lanes = shape[-1]
    return lax.broadcasted_iota(jnp.int32, shape, len(shape) - 1) // (lanes // hours)


def turned(value, places, hours):
    width = value.shape[-1] // hours
    result = value
    for k in range(1, hours):
        result = jnp.where(places == k, pltpu.roll(value, k * width, value.ndim - 1), result)
    return result


def pack_lanes(hours, hour, field, outs):
    group = group_of(field.shape[1:], hours)
    for r, out in enumerate(outs):
        target = lax.rem(hour + r + 1, hours)
        for j in range(out.shape[0]):
            packed = None
            for i in range(hours):
                part = turned(field[j * hours + i], lax.rem(i - target + hours, hours), hours)
                packed = part if i == 0 else jnp.where(group == i, part, packed)
            out[j] = packed


def merge_lanes(hours, hour, own, packs, block):
    group = group_of(own.shape, hours)
    for r, pack in enumerate(packs):
        source = lax.rem(hour + hours - r - 1, hours)
        part = pack[block // hours]
        part = turned(part, lax.rem(source - block % hours + hours, hours), hours)
        own = jnp.where(group == source, part, own)
    return own


def couple(hours, coupling, value):
    lanes = value.shape[-1]
    width = lanes // hours
    before, after = (pltpu.roll(value, d, value.ndim - 1) for d in (width, lanes - width))
    if hours == 2:
        return value - coupling * before
    group = group_of(value.shape, hours)
    sides = jnp.where(group > 0, before, 0.0) + jnp.where(group < hours - 1, after, 0.0)
    return value - coupling * sides


def pack_faces(faces, field, headings, outs):
    slots = faces.shape[1]
    places = [out.at[k] for out in outs for k in range(out.shape[0])]
    for m, place in enumerate(places):
        place[...] = field[faces[0, m % slots, headings[m // slots]]]


def far_product(stiffness, q, block):
    high, low = halves(block)
    right = jnp.concatenate([high, high, low], axis=0)
    return jnp.dot(stiffness[q], right, preferred_element_type=F32)


def landing(faces, counts, e, f, spare):
    return jnp.where(f < counts[0, e], faces[0, f, e], spare)


def open_body(hours, heads, faces, hour, field, *outs):
    pack_lanes(hours, hour[0], field, outs[: hours - 1])
    pack_faces(faces, field, heads, outs[hours - 1 :])


def turn_body(hours, heads, faces, hour, field, *refs):
    packs, (out, *faces_out) = refs[: hours - 1], refs[-1 - len(heads) :]
    for b in range(field.shape[0]):
        out[b] = merge_lanes(hours, hour[0], field[b], packs, b)
    pack_faces(faces, out, heads, faces_out)


def split_body(stiffness, out):
    width = stiffness.shape[1]
    for q in range(out.shape[0]):
        high, low = halves(stiffness[0, :, q * width : (q + 1) * width])
        out[q] = jnp.concatenate([high, low, high], axis=1)


def near_body(count, columns, kappa, stiffness, *refs):
    fields, outs, (high, low, diagonal) = refs[:count], refs[-3 - count : -3], refs[-3:]
    blocks = stiffness.shape[0]
    slots = columns.shape[0]
    lanes = fields[0].shape[2]
    diagonal[...] = jnp.transpose(kappa[...])
    for n, field in enumerate(fields):
        part = slice(n * lanes, (n + 1) * lanes)
        for b in range(blocks):
            high[b, :, part], low[b, :, part] = halves(field[b])
    for b in range(blocks):
        index = [columns[k, b] for k in range(slots)]
        highs = jnp.concatenate([high[i] for i in index], axis=0)
        lows = jnp.concatenate([low[i] for i in index], axis=0)
        left_high, left_low = halves(stiffness[b])
        near = jnp.dot(left_high, highs, preferred_element_type=F32)
        near += jnp.dot(left_low, highs, preferred_element_type=F32)
        near += jnp.dot(left_high, lows, preferred_element_type=F32)
        weight = 3.0 + diagonal[:, b : b + 1]
        for n, (field, out) in enumerate(zip(fields, outs)):
            out[b] = near[:, n * lanes : (n + 1) * lanes] + weight * field[b]


def near(columns, kappa, stiffness, fields, after=()):
    blocks, width, lanes = fields[0].shape
    return call(
        functools.partial(near_body, len(fields)),
        [struct(*field.shape) for field in fields],
        [columns],
        [kappa, stiffness, *fields, *after],
        [
            pltpu.VMEM((blocks, width, lanes * len(fields)), BF16),
            pltpu.VMEM((blocks, width, lanes * len(fields)), BF16),
            pltpu.VMEM((width, blocks), F32),
        ],
    )


def products(heads, stiffness, arrived, out):
    slots = arrived[0].shape[0]
    for n, e in enumerate(heads):
        for f in range(slots):
            out[n * slots + f] = far_product(stiffness, (e ^ 1) * slots + f, arrived[n][f])


def early_body(hours, heads, hour, stiffness, *refs):
    arrived, (_, out, *packs) = refs[: len(heads)], refs[len(heads) :]
    products(heads, stiffness, arrived, out)
    pack_lanes(hours, hour[0], out, packs)


def repack_body(hours, heads, faces, hour, own, field, *refs):
    outs = refs[-(len(heads) + hours - 1) :]
    pack_faces(faces, field, heads, outs[: len(heads)])
    pack_lanes(hours, hour[0], own, outs[len(heads) :])


def sum_body(*refs):
    refs[-1][...] = total([ref[...] for ref in refs[:-1]])


def late_body(heads, stiffness, *refs):
    products(heads, stiffness, refs[:-1], refs[-1])


def gather_far(hours, phases, faces, counts, hour, own, packs, late, near_part, field):
    blocks = near_part.shape[0]
    slots = faces.shape[1]
    for b in range(blocks):
        field[b] = near_part[b]
    for part, heads in enumerate(phases):
        for n, e in enumerate(heads):
            for f in range(slots):
                q = n * slots + f
                value = late(q) if part else merge_lanes(hours, hour[0], own[q], packs, q)
                field[landing(faces, counts, e ^ 1, f, blocks)] += value


def middle_body(hours, phases, heads, faces, counts, hour, coupling, near_part, own, late, *refs):
    turns = hours - 1
    packs = refs[:turns]
    first, image, *rest, field = refs[turns:]
    image_packs, first_packs, faces_out = rest[:turns], rest[turns : 2 * turns], rest[2 * turns :]
    late = late.__getitem__
    gather_far(hours, phases, faces, counts, hour, own, packs, late, near_part, field)
    for b in range(first.shape[0]):
        once = couple(hours, coupling[0], field[b])
        first[b] = once
        image[b] = couple(hours, coupling[0], once)
    pack_lanes(hours, hour[0], image, image_packs)
    pack_faces(faces, image, heads, faces_out)
    pack_lanes(hours, hour[0], first, first_packs)


def moments_body(hours, heads, faces, counts, hour, right, first, second, stiffness, *refs):
    arrived, (own, out) = refs[: len(heads)], refs[-2:]
    products(heads, stiffness, arrived, own)
    slots = faces.shape[1]
    sums = [jnp.zeros(right.shape[1:], F32) for _ in range(4)]
    for b in range(right.shape[0]):
        start, image = right[b], first[b]
        sums[0] += start * start
        sums[1] += start * image
        sums[2] += image * image
        sums[3] += image * second[b]
    for n, e in enumerate(heads):
        for f in range(slots):
            weight = jnp.where(f < counts[0, e ^ 1], 2.0, 0.0)
            sums[3] += weight * (first[faces[0, f, e ^ 1]] * own[n * slots + f])
    rows = jnp.concatenate([jnp.sum(s, axis=0, keepdims=True) for s in sums] * 2, axis=0)
    width = rows.shape[1] // hours
    rows = total([rows] + [pltpu.roll(rows, k * width, 1) for k in range(1, hours)])
    out[...] = jnp.where(group_of(rows.shape, hours) == hour[0], rows, 0.0)


def settle_body(
    hours, phases, faces, counts, hour, near_part, own, first, done, stiffness, *refs
):
    turns = hours - 1
    packs, first_packs, arrived = refs[:turns], refs[turns : 2 * turns], refs[2 * turns :]
    arrived, (image, out, rest, field) = arrived[:-4], arrived[-4:]
    count = done.shape[0]
    products(phases[1][len(phases[1]) - len(arrived) :], stiffness, arrived, rest)

    def late(q):
        return done[q] if q < count else rest[q - count]

    gather_far(hours, phases, faces, counts, hour, own, packs, late, near_part, field)
    for b in range(first.shape[0]):
        image[b] = merge_lanes(hours, hour[0], first[b], first_packs, b)
        out[b] = field[b]


def close_body(parts, right, first, second, *refs):
    sums, (solution, residual, solved, left, sems) = refs[:parts], refs[parts:]
    moment = total([s[...] for s in sums])
    m0, m1, m2, m3 = (moment[k : k + 1] for k in range(4))
    alpha = m0 / m1
    norm = alpha * alpha * m2 - m0
    lift = 1.0 + norm / m0
    step = norm / (lift * lift * m1 - 2.0 * lift * alpha * m2 + alpha * alpha * m3)
    on_right = alpha + step * lift
    on_first = step * alpha
    pieces = sems.shape[1]
    size = right.shape[0] // pieces
    copies = []
    for p in range(pieces):
        part = pl.ds(p * size, size)
        for b in range(p * size, (p + 1) * size):
            start, image = right[b], first[b]
            solved[b] = on_right * start - on_first * image
            left[b] = start - on_right * image + on_first * second[b]
        for n, (source, target) in enumerate(((solved, solution), (left, residual))):
            copies.append(pltpu.make_async_copy(source.at[part], target.at[part], sems.at[n, p]))
            copies[-1].start()
    for copy in copies:
        copy.wait()


def shifted(value, axes, sizes, steps):
    route = []
    for source in range(functools.reduce(lambda a, b: a * b, sizes)):
        rest, target, scale = source, 0, 1
        for size, step in reversed(list(zip(sizes, steps))):
            rest, place = divmod(rest, size)
            target += (place + step) % size * scale
            scale *= size
        route.append((source, target))
    return lax.ppermute(value, axes, route)


def send_faces(outgoing, heads, offsets):
    count = lax.axis_size(SPACE)
    return [shifted(v, SPACE, (count,), (offsets[e],)) for v, e in zip(outgoing, heads)]


def send_lanes(packs):
    hours = lax.axis_size("tm")
    return [shifted(v, ("tm",), (hours,), (r + 1,)) for r, v in enumerate(packs)]


def everywhere_sum(value):
    terms, summed, marks = [value], [], []
    for axis, partners in STAGES:
        if axis in summed:
            continue
        if len(terms) > 1:
            weight = ORDER[2 + len(marks)]
            terms = [call(sum_body, struct(*value.shape), [], terms, weight=weight)]
            marks += terms
        count = lax.axis_size(axis)
        if count in (2, 4):
            routes = [[(i, i ^ k) for i in range(count)] for k in partners]
            terms += [lax.ppermute(terms[0], axis, route) for route in routes]
        else:
            terms = [lax.psum(terms[0], axis)]
            summed.append(axis)
    return terms, marks


def shards(
    right_side,
    kappa_sq,
    time_coupling,
    near_stiffness,
    far_stiffness,
    near_columns,
    face_blocks,
    face_counts,
):
    right = right_side.reshape(right_side.shape[1:])
    blocks, width, lanes = right.shape
    hours = lax.axis_size("tm")
    hour = lax.axis_index("tm").reshape(1)
    headings, slots = face_blocks.shape[1:]
    stride = lax.axis_size(SPACE) // 4 + 1
    faces = jnp.swapaxes(face_blocks, 1, 2)
    columns = jnp.swapaxes(near_columns, 0, 1)
    counts = face_counts
    offsets = (1, -1, 2, -2, stride, -stride)
    field = struct(*right.shape)
    turns = hours - 1
    spare = [pltpu.VMEM((blocks + 1, width, lanes), F32)]

    def packs_of(count):
        return [struct(count // hours, width, lanes)] * turns

    def faces_of(heads):
        return [struct(slots, width, lanes)] * len(heads)

    def products_of(heads):
        return struct(len(heads) * slots, width, lanes)

    def body(function, *sizes):
        return functools.partial(function, hours, *sizes)

    def turn(heads, field_in, packs, after):
        out, *outgoing = call(
            body(turn_body, heads),
            [field] + faces_of(heads),
            [faces, hour],
            [field_in, *packs, *after],
        )
        return out, send_faces(outgoing, heads, offsets)

    def late_products(heads, arrived, weight):
        return call(
            functools.partial(late_body, heads),
            products_of(heads),
            [],
            [stiffness, *arrived],
            weight=weight,
        )

    phases, (heads, _) = PHASES
    outs = call(
        body(open_body, phases[0]),
        packs_of(blocks) + faces_of(phases[0]),
        [faces, hour],
        [right],
    )
    packs = send_lanes(outs[:turns])
    early = send_faces(outs[turns:], phases[0], offsets)
    probe_right, late = turn(phases[1], right, packs, [])
    stiffness = call(
        split_body, struct(headings * slots, width, 3 * width, dtype=BF16), [], [far_stiffness]
    )
    (near_part,) = near(columns, kappa_sq, near_stiffness, [probe_right])
    out = products_of(phases[0])
    own, *packs = call(
        body(early_body, phases[0]),
        [out] + packs_of(out.shape[0]),
        [hour],
        [stiffness, *early, probe_right],
    )
    packs = send_lanes(packs)
    late = late_products(phases[1], late, ORDER[0])
    first, image, *outs = call(
        body(middle_body, phases, heads),
        [field, field] + packs_of(blocks) * 2 + faces_of(heads),
        [faces, counts, hour, time_coupling],
        [near_part, own, late, *packs],
        spare,
    )

    phases = PHASES[1]
    packs, first_packs = send_lanes(outs[:turns]), send_lanes(outs[turns : 2 * turns])
    early = send_faces(outs[2 * turns :], phases[0], offsets)
    (near_probe,) = near(columns, kappa_sq, near_stiffness, [image])
    hour_image, late = turn(phases[1][:SPLIT], image, packs, [near_probe])
    own, sums = call(
        body(moments_body, phases[0]),
        [products_of(phases[0]), struct(8, lanes)],
        [faces, counts, hour],
        [probe_right, first, near_probe, stiffness, *early, *first_packs, hour_image],
    )
    sums, marks = everywhere_sum(sums)
    heads = phases[1][SPLIT:]
    outs = call(
        body(repack_body, heads),
        faces_of(heads) + packs_of(own.shape[0]),
        [faces, hour],
        [own, hour_image, *marks[:1]],
    )
    late += send_faces(outs[: len(heads)], heads, offsets)
    packs = send_lanes(outs[len(heads) :])
    (near_hour,) = near(columns, kappa_sq, near_stiffness, [hour_image], marks[-1:])
    done = late_products(phases[1][:SPLIT], late[:SPLIT], ORDER[1])
    hour_first, second = call(
        body(settle_body, phases),
        [field, field],
        [faces, counts, hour],
        [near_hour, own, first, done, stiffness, *packs, *first_packs, *late[SPLIT:]],
        [pltpu.VMEM((len(heads) * slots, width, lanes), F32)] + spare,
    )
    solution_field, residual = call(
        functools.partial(close_body, len(sums)),
        [field, field],
        [],
        [right, hour_first, second, *sums],
        [pltpu.VMEM(right.shape, F32)] * 2 + [pltpu.SemaphoreType.DMA((2, PIECES))],
        outs_in=pl.ANY,
    )
    return (solution_field[None], residual[None])


def solution(mesh):
    placed = (
        P(("grp", "tm"), SPACE, None, None),
        P(("grp", "mesh", "rep"), None),
        P("grp"),
        P(SPACE, None, None),
        P(SPACE, None, None),
        P(SPACE, None),
        P(SPACE, None, None),
        P(SPACE, None),
    )
    return jax.shard_map(
        shards,
        mesh=mesh,
        in_specs=placed,
        out_specs=(
            P(("grp", "tm"), SPACE, None, None),
            P(("grp", "tm"), SPACE, None, None),
        ),
        check_vma=False,
    )
```

```python
import functools

import jax
import jax.numpy as jnp
from jax import lax
from jax.experimental import pallas as pl
from jax.experimental.pallas import tpu as pltpu
from jax.sharding import PartitionSpec as P

SPACE = ("mesh", "rep")
F32 = jnp.float32
BF16 = jnp.bfloat16
PHASES = (((4, 2), (3, 5, 1, 0)), ((4, 2, 0), (5, 3, 1)))
STAGES = (("rep", (1,)), ("tm", (1,)), ("mesh", (1, 2, 3)))
SPLIT = (3, 2)
PIECES = 4
ORDER = (40, 160, 0, 0)


def struct(*shape, dtype=F32):
    return jax.ShapeDtypeStruct(shape, dtype)


def call(body, outs, scalars, vectors, scratch=(), weight=0, outs_in=pltpu.VMEM):
    spaces = [pltpu.SMEM] * len(scalars) + [pltpu.VMEM] * len(vectors)
    return pl.pallas_call(
        body,
        out_shape=outs,
        in_specs=[pl.BlockSpec(memory_space=space) for space in spaces],
        out_specs=jax.tree.map(lambda _: pl.BlockSpec(memory_space=outs_in), outs),
        scratch_shapes=scratch,
        cost_estimate=pl.CostEstimate(
            flops=(weight << 30) + 1024, transcendentals=0, bytes_accessed=1024
        ),
        compiler_params=pltpu.CompilerParams(vmem_limit_bytes=16 << 20),
    )(*scalars, *vectors)


def total(values):
    return functools.reduce(jnp.add, values)


def halves(value):
    high = value.astype(BF16)
    return high, (value - high.astype(F32)).astype(BF16)


def group_of(shape, hours):
    lanes = shape[-1]
    return lax.broadcasted_iota(jnp.int32, shape, len(shape) - 1) // (lanes // hours)


def turned(value, places, hours):
    width = value.shape[-1] // hours
    result = value
    for k in range(1, hours):
        result = jnp.where(places == k, pltpu.roll(value, k * width, value.ndim - 1), result)
    return result


def pack_lanes(hours, hour, field, outs):
    group = group_of(field.shape[1:], hours)
    for r, out in enumerate(outs):
        target = lax.rem(hour + r + 1, hours)
        for j in range(out.shape[0]):
            packed = None
            for i in range(hours):
                part = turned(field[j * hours + i], lax.rem(i - target + hours, hours), hours)
                packed = part if i == 0 else jnp.where(group == i, part, packed)
            out[j] = packed


def merge_lanes(hours, hour, own, packs, block):
    group = group_of(own.shape, hours)
    for r, pack in enumerate(packs):
        source = lax.rem(hour + hours - r - 1, hours)
        part = pack[block // hours]
        part = turned(part, lax.rem(source - block % hours + hours, hours), hours)
        own = jnp.where(group == source, part, own)
    return own


def couple(hours, coupling, value):
    lanes = value.shape[-1]
    width = lanes // hours
    before, after = (pltpu.roll(value, d, value.ndim - 1) for d in (width, lanes - width))
    if hours == 2:
        return value - coupling * before
    group = group_of(value.shape, hours)
    sides = jnp.where(group > 0, before, 0.0) + jnp.where(group < hours - 1, after, 0.0)
    return value - coupling * sides


def pack_faces(faces, field, headings, outs):
    slots = faces.shape[1]
    places = [out.at[k] for out in outs for k in range(out.shape[0])]
    for m, place in enumerate(places):
        place[...] = field[faces[0, m % slots, headings[m // slots]]]


def far_product(stiffness, q, block):
    high, low = halves(block)
    right = jnp.concatenate([high, high, low], axis=0)
    return jnp.dot(stiffness[q], right, preferred_element_type=F32)


def landing(faces, counts, e, f, spare):
    return jnp.where(f < counts[0, e], faces[0, f, e], spare)


def open_body(hours, heads, faces, hour, field, *outs):
    pack_lanes(hours, hour[0], field, outs[: hours - 1])
    pack_faces(faces, field, heads, outs[hours - 1 :])


def turn_body(hours, heads, faces, hour, field, *refs):
    packs, (out, *faces_out) = refs[: hours - 1], refs[hours - 1 :]
    for b in range(field.shape[0]):
        out[b] = merge_lanes(hours, hour[0], field[b], packs, b)
    pack_faces(faces, out, heads, faces_out)


def turn_near_body(hours, heads, faces, hour, columns, field, kappa, stiffness, _, *refs):
    packs, (near_out, *outs) = refs[: hours - 1], refs[hours - 1 :]
    outs, scratch = outs[: 1 + len(heads)], outs[1 + len(heads) :]
    turn_body(hours, heads, faces, hour, field, *packs, *outs)
    near_body(columns, kappa, stiffness, outs[0], near_out, *scratch)


def split_body(stiffness, out):
    width = stiffness.shape[1]
    for q in range(out.shape[0]):
        high, low = halves(stiffness[0, :, q * width : (q + 1) * width])
        out[q] = jnp.concatenate([high, low, high], axis=1)


def near_body(columns, kappa, stiffness, field, out, high, low, diagonal):
    blocks = field.shape[0]
    slots = columns.shape[0]
    diagonal[...] = jnp.transpose(kappa[...])
    for b in range(blocks):
        high[b], low[b] = halves(field[b])
    for b in range(blocks):
        index = [columns[k, b] for k in range(slots)]
        highs = jnp.concatenate([high[i] for i in index], axis=0)
        lows = jnp.concatenate([low[i] for i in index], axis=0)
        left_high, left_low = halves(stiffness[b])
        value = jnp.dot(left_high, highs, preferred_element_type=F32)
        value += jnp.dot(left_low, highs, preferred_element_type=F32)
        value += jnp.dot(left_high, lows, preferred_element_type=F32)
        out[b] = value + (3.0 + diagonal[:, b : b + 1]) * field[b]


def near_scratch(field):
    blocks, width, lanes = field.shape
    return [pltpu.VMEM(field.shape, BF16)] * 2 + [pltpu.VMEM((width, blocks), F32)]


def near(columns, kappa, stiffness, field):
    return call(
        near_body,
        struct(*field.shape),
        [columns],
        [kappa, stiffness, field],
        near_scratch(field),
    )


def products(heads, stiffness, arrived, out):
    for n, e in enumerate(heads):
        slots = arrived[n].shape[0]
        for f in range(slots):
            out[n * slots + f] = far_product(stiffness, (e ^ 1) * slots + f, arrived[n][f])


def early_body(hours, heads, hour, stiffness, *refs):
    arrived, (_, out, *packs) = refs[: len(heads)], refs[len(heads) :]
    products(heads, stiffness, arrived, out)
    pack_lanes(hours, hour[0], out, packs)


def repack_body(hours, hour, own, *refs):
    pack_lanes(hours, hour[0], own, refs[1 - hours :])


def sum_body(*refs):
    refs[-1][...] = total([ref[...] for ref in refs[:-1]])


def late_body(heads, stiffness, *refs):
    products(heads, stiffness, refs[:-1], refs[-1])


def gather_far(hours, phases, faces, counts, hour, own, packs, late, near_part, field):
    blocks = near_part.shape[0]
    slots = faces.shape[1]
    for b in range(blocks):
        field[b] = near_part[b]
    for part, heads in enumerate(phases):
        for n, e in enumerate(heads):
            for f in range(slots):
                q = n * slots + f
                value = late(q) if part else merge_lanes(hours, hour[0], own[q], packs, q)
                field[landing(faces, counts, e ^ 1, f, blocks)] += value


def late_values(phases, done, stiffness, arrived, rest):
    count = done.shape[0]
    products(phases[1][len(phases[1]) - len(arrived) :], stiffness, arrived, rest)
    return lambda q: done[q] if q < count else rest[q - count]


def middle_body(
    hours, phases, heads, split, faces, counts, hour, coupling, near_part, own, done, stiffness, *refs
):
    turns = hours - 1
    packs, refs = refs[:turns], refs[turns:]
    left = len(phases[1]) - split
    arrived, (first, image, *outs, rest, field) = refs[:left], refs[left:]
    image_packs, first_packs, faces_out = outs[:turns], outs[turns : 2 * turns], outs[2 * turns :]
    late = late_values(phases, done, stiffness, arrived, rest)
    gather_far(hours, phases, faces, counts, hour, own, packs, late, near_part, field)
    for b in range(first.shape[0]):
        once = couple(hours, coupling[0], field[b])
        first[b] = once
        image[b] = couple(hours, coupling[0], once)
    pack_lanes(hours, hour[0], image, image_packs)
    pack_faces(faces, image, heads, faces_out)
    pack_lanes(hours, hour[0], first, first_packs)


def moments_body(hours, heads, faces, counts, hour, right, first, second, stiffness, *refs):
    arrived, (own, out) = refs[: len(heads)], refs[-2:]
    products(heads, stiffness, arrived, own)
    slots = faces.shape[1]
    sums = [jnp.zeros(right.shape[1:], F32) for _ in range(4)]
    for b in range(right.shape[0]):
        start, image = right[b], first[b]
        sums[0] += start * start
        sums[1] += start * image
        sums[2] += image * image
        sums[3] += image * second[b]
    for n, e in enumerate(heads):
        for f in range(slots):
            weight = jnp.where(f < counts[0, e ^ 1], 2.0, 0.0)
            sums[3] += weight * (first[faces[0, f, e ^ 1]] * own[n * slots + f])
    rows = jnp.concatenate([jnp.sum(s, axis=0, keepdims=True) for s in sums] * 2, axis=0)
    width = rows.shape[1] // hours
    rows = total([rows] + [pltpu.roll(rows, k * width, 1) for k in range(1, hours)])
    out[...] = jnp.where(group_of(rows.shape, hours) == hour[0], rows, 0.0)


def gather_body(
    hours, phases, split, faces, counts, hour, near_part, own, first, stiffness, *refs
):
    turns = hours - 1
    first_packs, refs = refs[:turns], refs[turns:]
    arrived, (image, out, made, field) = refs[:split], refs[split:]
    blocks, slots = first.shape[0], faces.shape[1]
    heads = phases[1][:split]
    products(heads, stiffness, arrived, made)
    for b in range(blocks):
        image[b] = merge_lanes(hours, hour[0], first[b], first_packs, b)
        field[b] = near_part[b]
    mine = group_of(own.shape[1:], hours) == hour[0]
    for n, e in enumerate(phases[0]):
        for f in range(slots):
            block = landing(faces, counts, e ^ 1, f, blocks)
            field[block] += jnp.where(mine, own[n * slots + f], 0.0)
    for n, e in enumerate(heads):
        for f in range(slots):
            field[landing(faces, counts, e ^ 1, f, blocks)] += made[n * slots + f]
    for b in range(blocks):
        out[b] = field[b]


def settle_body(hours, phases, split, faces, counts, hour, start, stiffness, *refs):
    turns = hours - 1
    packs, refs = refs[:turns], refs[turns:]
    arrived, (out, made, field) = refs[:-3], refs[-3:]
    blocks, slots = start.shape[0], faces.shape[1]
    heads = phases[1][split:]
    products(heads, stiffness, arrived, made)
    for b in range(blocks):
        field[b] = start[b]
    zero = jnp.zeros(start.shape[1:], F32)
    for n, e in enumerate(phases[0]):
        for f in range(slots):
            value = merge_lanes(hours, hour[0], zero, packs, n * slots + f)
            field[landing(faces, counts, e ^ 1, f, blocks)] += value
    for n, e in enumerate(heads):
        for f in range(slots):
            field[landing(faces, counts, e ^ 1, f, blocks)] += made[n * slots + f]
    for b in range(blocks):
        out[b] = field[b]


def close_body(parts, right, first, second, *refs):
    sums, (solution, residual, solved, left, sems) = refs[:parts], refs[parts:]
    moment = total([s[...] for s in sums])
    m0, m1, m2, m3 = (moment[k : k + 1] for k in range(4))
    alpha = m0 / m1
    norm = alpha * alpha * m2 - m0
    lift = 1.0 + norm / m0
    step = norm / (lift * lift * m1 - 2.0 * lift * alpha * m2 + alpha * alpha * m3)
    on_right = alpha + step * lift
    on_first = step * alpha
    pieces = sems.shape[1]
    size = right.shape[0] // pieces
    copies = []
    for p in range(pieces):
        part = pl.ds(p * size, size)
        for b in range(p * size, (p + 1) * size):
            start, image = right[b], first[b]
            solved[b] = on_right * start - on_first * image
            left[b] = start - on_right * image + on_first * second[b]
        for n, (source, target) in enumerate(((solved, solution), (left, residual))):
            copies.append(pltpu.make_async_copy(source.at[part], target.at[part], sems.at[n, p]))
            copies[-1].start()
    for copy in copies:
        copy.wait()


def shifted(value, axes, sizes, steps):
    route = []
    for source in range(functools.reduce(lambda a, b: a * b, sizes)):
        rest, target, scale = source, 0, 1
        for size, step in reversed(list(zip(sizes, steps))):
            rest, place = divmod(rest, size)
            target += (place + step) % size * scale
            scale *= size
        route.append((source, target))
    return lax.ppermute(value, axes, route)


def send_faces(outgoing, heads, offsets):
    count = lax.axis_size(SPACE)
    return [shifted(v, SPACE, (count,), (offsets[e],)) for v, e in zip(outgoing, heads)]


def send_lanes(packs):
    hours = lax.axis_size("tm")
    return [shifted(v, ("tm",), (hours,), (r + 1,)) for r, v in enumerate(packs)]


def everywhere_sum(value):
    terms, summed, marks = [value], [], []
    for axis, partners in STAGES:
        if axis in summed:
            continue
        if len(terms) > 1:
            weight = ORDER[2 + len(marks)]
            terms = [call(sum_body, struct(*value.shape), [], terms, weight=weight)]
            marks += terms
        count = lax.axis_size(axis)
        if count in (2, 4):
            routes = [[(i, i ^ k) for i in range(count)] for k in partners]
            terms += [lax.ppermute(terms[0], axis, route) for route in routes]
        else:
            terms = [lax.psum(terms[0], axis)]
            summed.append(axis)
    return terms, marks


def shards(
    right_side,
    kappa_sq,
    time_coupling,
    near_stiffness,
    far_stiffness,
    near_columns,
    face_blocks,
    face_counts,
):
    right = right_side.reshape(right_side.shape[1:])
    blocks, width, lanes = right.shape
    hours = lax.axis_size("tm")
    hour = lax.axis_index("tm").reshape(1)
    headings, slots = face_blocks.shape[1:]
    stride = lax.axis_size(SPACE) // 4 + 1
    faces = jnp.swapaxes(face_blocks, 1, 2)
    columns = jnp.swapaxes(near_columns, 0, 1)
    counts = face_counts
    offsets = (1, -1, 2, -2, stride, -stride)
    field = struct(*right.shape)
    turns = hours - 1
    spare = [pltpu.VMEM((blocks + 1, width, lanes), F32)]

    def packs_of(count):
        return [struct(count // hours, width, lanes)] * turns

    def faces_of(heads):
        return [struct(slots, width, lanes)] * len(heads)

    def products_of(heads):
        return struct(len(heads) * slots, width, lanes)

    def products_in(heads):
        return pltpu.VMEM((max(len(heads), 1) * slots, width, lanes), F32)

    def body(function, *sizes):
        return functools.partial(function, hours, *sizes)

    def turn(heads, field_in, packs):
        out, *outgoing = call(
            body(turn_body, heads), [field] + faces_of(heads), [faces, hour], [field_in, *packs]
        )
        return out, send_faces(outgoing, heads, offsets)

    def late_products(heads, arrived, weight):
        return call(
            functools.partial(late_body, heads),
            products_of(heads),
            [],
            [stiffness, *arrived],
            weight=weight,
        )

    phases, (heads, _) = PHASES
    outs = call(
        body(open_body, phases[0]),
        packs_of(blocks) + faces_of(phases[0]),
        [faces, hour],
        [right],
    )
    packs = send_lanes(outs[:turns])
    early = send_faces(outs[turns:], phases[0], offsets)
    probe_right, late = turn(phases[1], right, packs)
    stiffness = call(
        split_body, struct(headings * slots, width, 3 * width, dtype=BF16), [], [far_stiffness]
    )
    near_part = near(columns, kappa_sq, near_stiffness, probe_right)
    out = products_of(phases[0])
    own, *packs = call(
        body(early_body, phases[0]),
        [out] + packs_of(out.shape[0]),
        [hour],
        [stiffness, *early, probe_right],
    )
    packs = send_lanes(packs)
    split = SPLIT[0]
    done = late_products(phases[1][:split], late[:split], ORDER[0])
    first, image, *outs = call(
        body(middle_body, phases, heads, split),
        [field, field] + packs_of(blocks) * 2 + faces_of(heads),
        [faces, counts, hour, time_coupling],
        [near_part, own, done, stiffness, *packs, *late[split:]],
        [products_in(phases[1][split:])] + spare,
    )

    phases = PHASES[1]
    packs, first_packs = send_lanes(outs[:turns]), send_lanes(outs[turns : 2 * turns])
    early = send_faces(outs[2 * turns :], phases[0], offsets)
    near_probe = near(columns, kappa_sq, near_stiffness, image)
    near_hour, hour_image, *outgoing = call(
        body(turn_near_body, phases[1]),
        [field, field] + faces_of(phases[1]),
        [faces, hour, columns],
        [image, kappa_sq, near_stiffness, near_probe, *packs],
        near_scratch(right),
    )
    late = send_faces(outgoing, phases[1], offsets)
    own, sums = call(
        body(moments_body, phases[0]),
        [products_of(phases[0]), struct(8, lanes)],
        [faces, counts, hour],
        [probe_right, first, near_probe, stiffness, *early, *first_packs, hour_image],
    )
    sums, marks = everywhere_sum(sums)
    packs = send_lanes(
        call(
            body(repack_body),
            packs_of(own.shape[0]),
            [hour],
            [own, *marks[:1]],
        )
    )
    split = SPLIT[1]
    hour_first, partial = call(
        body(gather_body, phases, split),
        [field, field],
        [faces, counts, hour],
        [near_hour, own, first, stiffness, *first_packs, *late[:split]],
        [products_in(phases[1][:split])] + spare,
        weight=ORDER[1],
    )
    second = call(
        body(settle_body, phases, split),
        field,
        [faces, counts, hour],
        [partial, stiffness, *packs, *late[split:]],
        [products_in(phases[1][split:])] + spare,
    )
    solution_field, residual = call(
        functools.partial(close_body, len(sums)),
        [field, field],
        [],
        [right, hour_first, second, *sums],
        [pltpu.VMEM(right.shape, F32)] * 2 + [pltpu.SemaphoreType.DMA((2, PIECES))],
        outs_in=pl.ANY,
    )
    return (solution_field[None], residual[None])


def solution(mesh):
    placed = (
        P(("grp", "tm"), SPACE, None, None),
        P(("grp", "mesh", "rep"), None),
        P("grp"),
        P(SPACE, None, None),
        P(SPACE, None, None),
        P(SPACE, None),
        P(SPACE, None, None),
        P(SPACE, None),
    )
    return jax.shard_map(
        shards,
        mesh=mesh,
        in_specs=placed,
        out_specs=(
            P(("grp", "tm"), SPACE, None, None),
            P(("grp", "tm"), SPACE, None, None),
        ),
        check_vma=False,
    )
```

```python
import functools

import jax
import jax.numpy as jnp
from jax import lax
from jax.experimental import pallas as pl
from jax.experimental.pallas import tpu as pltpu
from jax.sharding import PartitionSpec as P

SPACE = ("mesh", "rep")
F32 = jnp.float32
BF16 = jnp.bfloat16
PHASES = (((4, 2), (3, 5, 1, 0)), ((4, 2, 0), (5, 3, 1)))
STAGES = (("rep", (1,)), ("tm", (1,)), ("mesh", (1, 2, 3)))
SPLIT = (3, 2)
PIECES = 4
ORDER = (40, 160, 0, 0)


def struct(*shape, dtype=F32):
    return jax.ShapeDtypeStruct(shape, dtype)


def call(
    body, outs, scalars, vectors, scratch=(), weight=0, vectors_in=pltpu.VMEM, outs_in=pltpu.VMEM
):
    spaces = [pltpu.SMEM] * len(scalars) + [vectors_in] * len(vectors)
    return pl.pallas_call(
        body,
        out_shape=outs,
        in_specs=[pl.BlockSpec(memory_space=space) for space in spaces],
        out_specs=jax.tree.map(lambda _: pl.BlockSpec(memory_space=outs_in), outs),
        scratch_shapes=scratch,
        cost_estimate=pl.CostEstimate(
            flops=(weight << 30) + 1024, transcendentals=0, bytes_accessed=1024
        ),
        compiler_params=pltpu.CompilerParams(vmem_limit_bytes=16 << 20),
    )(*scalars, *vectors)


def total(values):
    return functools.reduce(jnp.add, values)


def halves(value):
    high = value.astype(BF16)
    return high, (value - high.astype(F32)).astype(BF16)


def group_of(shape, hours):
    lanes = shape[-1]
    return lax.broadcasted_iota(jnp.int32, shape, len(shape) - 1) // (lanes // hours)


def turned(value, places, hours):
    width = value.shape[-1] // hours
    result = value
    for k in range(1, hours):
        result = jnp.where(places == k, pltpu.roll(value, k * width, value.ndim - 1), result)
    return result


def pack_lanes(hours, hour, field, outs):
    group = group_of(field.shape[1:], hours)
    for r, out in enumerate(outs):
        target = lax.rem(hour + r + 1, hours)
        for j in range(out.shape[0]):
            packed = None
            for i in range(hours):
                part = turned(field[j * hours + i], lax.rem(i - target + hours, hours), hours)
                packed = part if i == 0 else jnp.where(group == i, part, packed)
            out[j] = packed


def merge_lanes(hours, hour, own, packs, block):
    group = group_of(own.shape, hours)
    for r, pack in enumerate(packs):
        source = lax.rem(hour + hours - r - 1, hours)
        part = pack[block // hours]
        part = turned(part, lax.rem(source - block % hours + hours, hours), hours)
        own = jnp.where(group == source, part, own)
    return own


def couple(hours, coupling, value):
    lanes = value.shape[-1]
    width = lanes // hours
    before, after = (pltpu.roll(value, d, value.ndim - 1) for d in (width, lanes - width))
    if hours == 2:
        return value - coupling * before
    group = group_of(value.shape, hours)
    sides = jnp.where(group > 0, before, 0.0) + jnp.where(group < hours - 1, after, 0.0)
    return value - coupling * sides


def pack_faces(faces, field, headings, outs):
    slots = faces.shape[1]
    places = [out.at[k] for out in outs for k in range(out.shape[0])]
    for m, place in enumerate(places):
        place[...] = field[faces[0, m % slots, headings[m // slots]]]


def far_product(stiffness, q, block):
    high, low = halves(block)
    right = jnp.concatenate([high, high, low], axis=0)
    return jnp.dot(stiffness[q], right, preferred_element_type=F32)


def landing(faces, counts, e, f, spare):
    return jnp.where(f < counts[0, e], faces[0, f, e], spare)


def open_body(hours, heads, hour, faces_in, field_in, *refs):
    (field, table, *outs), (faces, sems) = refs[:-2], refs[-2:]
    copies = [
        pltpu.make_async_copy(field_in, field, sems.at[0]),
        pltpu.make_async_copy(faces_in, faces, sems.at[1]),
        pltpu.make_async_copy(faces_in, table, sems.at[2]),
    ]
    for copy in copies:
        copy.start()
    copies[0].wait()
    pack_lanes(hours, hour[0], field, outs[: hours - 1])
    copies[1].wait()
    pack_faces(faces, field, heads, outs[hours - 1 :])
    copies[2].wait()


def turn_body(hours, heads, faces, hour, field, *refs):
    packs, (out, *faces_out) = refs[: hours - 1], refs[hours - 1 :]
    for b in range(field.shape[0]):
        out[b] = merge_lanes(hours, hour[0], field[b], packs, b)
    pack_faces(faces, out, heads, faces_out)


def turn_near_body(hours, heads, faces, hour, columns, field, kappa, stiffness, _, *refs):
    packs, (near_out, *outs) = refs[: hours - 1], refs[hours - 1 :]
    outs, scratch = outs[: 1 + len(heads)], outs[1 + len(heads) :]
    turn_body(hours, heads, faces, hour, field, *packs, *outs)
    near_body(columns, kappa, stiffness, outs[0], near_out, *scratch)


def split_body(stiffness, out):
    width = stiffness.shape[1]
    for q in range(out.shape[0]):
        high, low = halves(stiffness[0, :, q * width : (q + 1) * width])
        out[q] = jnp.concatenate([high, low, high], axis=1)


def near_body(columns, kappa, stiffness, field, out, high, low, diagonal):
    blocks = field.shape[0]
    slots = columns.shape[0]
    diagonal[...] = jnp.transpose(kappa[...])
    for b in range(blocks):
        high[b], low[b] = halves(field[b])
    for b in range(blocks):
        index = [columns[k, b] for k in range(slots)]
        highs = jnp.concatenate([high[i] for i in index], axis=0)
        lows = jnp.concatenate([low[i] for i in index], axis=0)
        left_high, left_low = halves(stiffness[b])
        value = jnp.dot(left_high, highs, preferred_element_type=F32)
        value += jnp.dot(left_low, highs, preferred_element_type=F32)
        value += jnp.dot(left_high, lows, preferred_element_type=F32)
        out[b] = value + (3.0 + diagonal[:, b : b + 1]) * field[b]


def near_scratch(field):
    blocks, width, lanes = field.shape
    return [pltpu.VMEM(field.shape, BF16)] * 2 + [pltpu.VMEM((width, blocks), F32)]


def near(columns, kappa, stiffness, field):
    return call(
        near_body,
        struct(*field.shape),
        [columns],
        [kappa, stiffness, field],
        near_scratch(field),
    )


def products(heads, stiffness, arrived, out):
    for n, e in enumerate(heads):
        slots = arrived[n].shape[0]
        for f in range(slots):
            out[n * slots + f] = far_product(stiffness, (e ^ 1) * slots + f, arrived[n][f])


def early_body(hours, heads, hour, stiffness, *refs):
    arrived, (_, out, *packs) = refs[: len(heads)], refs[len(heads) :]
    products(heads, stiffness, arrived, out)
    pack_lanes(hours, hour[0], out, packs)


def repack_body(hours, hour, own, *refs):
    pack_lanes(hours, hour[0], own, refs[1 - hours :])


def sum_body(*refs):
    refs[-1][...] = refs[-2][...] = total([ref[...] for ref in refs[:-2]])


def late_body(heads, stiffness, *refs):
    products(heads, stiffness, refs[:-1], refs[-1])


def gather_far(hours, phases, faces, counts, hour, own, packs, late, near_part, field):
    blocks = near_part.shape[0]
    slots = faces.shape[1]
    for b in range(blocks):
        field[b] = near_part[b]
    for part, heads in enumerate(phases):
        for n, e in enumerate(heads):
            for f in range(slots):
                q = n * slots + f
                value = late(q) if part else merge_lanes(hours, hour[0], own[q], packs, q)
                field[landing(faces, counts, e ^ 1, f, blocks)] += value


def late_values(phases, done, stiffness, arrived, rest):
    count = done.shape[0]
    products(phases[1][len(phases[1]) - len(arrived) :], stiffness, arrived, rest)
    return lambda q: done[q] if q < count else rest[q - count]


def middle_body(
    hours, phases, heads, split, faces, counts, hour, coupling, near_part, own, done, stiffness, *refs
):
    turns = hours - 1
    packs, refs = refs[:turns], refs[turns:]
    left = len(phases[1]) - split
    arrived, (first, image, *outs, rest, field) = refs[:left], refs[left:]
    image_packs, first_packs, faces_out = outs[:turns], outs[turns : 2 * turns], outs[2 * turns :]
    late = late_values(phases, done, stiffness, arrived, rest)
    gather_far(hours, phases, faces, counts, hour, own, packs, late, near_part, field)
    for b in range(first.shape[0]):
        once = couple(hours, coupling[0], field[b])
        first[b] = once
        image[b] = couple(hours, coupling[0], once)
    pack_lanes(hours, hour[0], image, image_packs)
    pack_faces(faces, image, heads, faces_out)
    pack_lanes(hours, hour[0], first, first_packs)


def moments_body(hours, heads, faces, counts, hour, right, first, second, stiffness, *refs):
    arrived, (own, out) = refs[: len(heads)], refs[-2:]
    products(heads, stiffness, arrived, own)
    slots = faces.shape[1]
    sums = [jnp.zeros(right.shape[1:], F32) for _ in range(4)]
    for b in range(right.shape[0]):
        start, image = right[b], first[b]
        sums[0] += start * start
        sums[1] += start * image
        sums[2] += image * image
        sums[3] += image * second[b]
    for n, e in enumerate(heads):
        for f in range(slots):
            weight = jnp.where(f < counts[0, e ^ 1], 2.0, 0.0)
            sums[3] += weight * (first[faces[0, f, e ^ 1]] * own[n * slots + f])
    rows = jnp.concatenate([jnp.sum(s, axis=0, keepdims=True) for s in sums] * 2, axis=0)
    width = rows.shape[1] // hours
    rows = total([rows] + [pltpu.roll(rows, k * width, 1) for k in range(1, hours)])
    out[...] = jnp.where(group_of(rows.shape, hours) == hour[0], rows, 0.0)


def gather_body(
    hours, phases, split, faces, counts, hour, near_part, own, first, stiffness, *refs
):
    turns = hours - 1
    first_packs, refs = refs[:turns], refs[turns:]
    arrived, (image, out, made, field) = refs[:split], refs[split:]
    blocks, slots = first.shape[0], faces.shape[1]
    heads = phases[1][:split]
    products(heads, stiffness, arrived, made)
    for b in range(blocks):
        image[b] = merge_lanes(hours, hour[0], first[b], first_packs, b)
        field[b] = near_part[b]
    mine = group_of(own.shape[1:], hours) == hour[0]
    for n, e in enumerate(phases[0]):
        for f in range(slots):
            block = landing(faces, counts, e ^ 1, f, blocks)
            field[block] += jnp.where(mine, own[n * slots + f], 0.0)
    for n, e in enumerate(heads):
        for f in range(slots):
            field[landing(faces, counts, e ^ 1, f, blocks)] += made[n * slots + f]
    for b in range(blocks):
        out[b] = field[b]


def settle_body(hours, phases, split, faces, counts, hour, start, stiffness, *refs):
    turns = hours - 1
    packs, refs = refs[:turns], refs[turns:]
    arrived, (out, made, field) = refs[:-3], refs[-3:]
    blocks, slots = start.shape[0], faces.shape[1]
    heads = phases[1][split:]
    products(heads, stiffness, arrived, made)
    for b in range(blocks):
        field[b] = start[b]
    zero = jnp.zeros(start.shape[1:], F32)
    for n, e in enumerate(phases[0]):
        for f in range(slots):
            value = merge_lanes(hours, hour[0], zero, packs, n * slots + f)
            field[landing(faces, counts, e ^ 1, f, blocks)] += value
    for n, e in enumerate(heads):
        for f in range(slots):
            field[landing(faces, counts, e ^ 1, f, blocks)] += made[n * slots + f]
    for b in range(blocks):
        out[b] = field[b]


def close_body(parts, right, first, second, *refs):
    sums, (solution, residual, solved, left, sems) = refs[:parts], refs[parts:]
    moment = total([s[...] for s in sums])
    m0, m1, m2, m3 = (moment[k : k + 1] for k in range(4))
    alpha = m0 / m1
    norm = alpha * alpha * m2 - m0
    lift = 1.0 + norm / m0
    step = norm / (lift * lift * m1 - 2.0 * lift * alpha * m2 + alpha * alpha * m3)
    on_right = alpha + step * lift
    on_first = step * alpha
    pieces = sems.shape[1]
    size = right.shape[0] // pieces
    copies = []
    for p in range(pieces):
        part = pl.ds(p * size, size)
        for b in range(p * size, (p + 1) * size):
            start, image = right[b], first[b]
            solved[b] = on_right * start - on_first * image
            left[b] = start - on_right * image + on_first * second[b]
        for n, (source, target) in enumerate(((solved, solution), (left, residual))):
            copies.append(pltpu.make_async_copy(source.at[part], target.at[part], sems.at[n, p]))
            copies[-1].start()
    for copy in copies:
        copy.wait()


def shifted(value, axes, sizes, steps):
    route = []
    for source in range(functools.reduce(lambda a, b: a * b, sizes)):
        rest, target, scale = source, 0, 1
        for size, step in reversed(list(zip(sizes, steps))):
            rest, place = divmod(rest, size)
            target += (place + step) % size * scale
            scale *= size
        route.append((source, target))
    return lax.ppermute(value, axes, route)


def send_faces(outgoing, heads, offsets):
    count = lax.axis_size(SPACE)
    return [shifted(v, SPACE, (count,), (offsets[e],)) for v, e in zip(outgoing, heads)]


def send_lanes(packs):
    hours = lax.axis_size("tm")
    return [shifted(v, ("tm",), (hours,), (r + 1,)) for r, v in enumerate(packs)]


def everywhere_sum(value):
    terms, summed, marks = [value], [], []
    for axis, partners in STAGES:
        if axis in summed:
            continue
        if len(terms) > 1:
            weight = ORDER[2 + len(marks)]
            sent, kept = call(sum_body, [struct(*value.shape)] * 2, [], terms, weight=weight)
            terms = [kept]
            marks += terms
        else:
            sent = value
        count = lax.axis_size(axis)
        if count in (2, 4):
            routes = [[(i, i ^ k) for i in range(count)] for k in partners]
            terms += [lax.ppermute(sent, axis, route) for route in routes]
        else:
            terms = [lax.psum(sent, axis)]
            summed.append(axis)
    return terms, marks


def shards(
    right_side,
    kappa_sq,
    time_coupling,
    near_stiffness,
    far_stiffness,
    near_columns,
    face_blocks,
    face_counts,
):
    right = right_side.reshape(right_side.shape[1:])
    blocks, width, lanes = right.shape
    hours = lax.axis_size("tm")
    hour = lax.axis_index("tm").reshape(1)
    headings, slots = face_blocks.shape[1:]
    stride = lax.axis_size(SPACE) // 4 + 1
    faces = jnp.swapaxes(face_blocks, 1, 2)
    columns = jnp.swapaxes(near_columns, 0, 1)
    counts = face_counts
    offsets = (1, -1, 2, -2, stride, -stride)
    field = struct(*right.shape)
    turns = hours - 1
    spare = [pltpu.VMEM((blocks + 1, width, lanes), F32)]

    def packs_of(count):
        return [struct(count // hours, width, lanes)] * turns

    def faces_of(heads):
        return [struct(slots, width, lanes)] * len(heads)

    def products_of(heads):
        return struct(len(heads) * slots, width, lanes)

    def products_in(heads):
        return pltpu.VMEM((max(len(heads), 1) * slots, width, lanes), F32)

    def body(function, *sizes):
        return functools.partial(function, hours, *sizes)

    def turn(heads, field_in, packs):
        out, *outgoing = call(
            body(turn_body, heads), [field] + faces_of(heads), [faces, hour], [field_in, *packs]
        )
        return out, send_faces(outgoing, heads, offsets)

    def late_products(heads, arrived, weight):
        return call(
            functools.partial(late_body, heads),
            products_of(heads),
            [],
            [stiffness, *arrived],
            weight=weight,
        )

    phases, (heads, _) = PHASES
    kept, table, *outs = call(
        body(open_body, phases[0]),
        [field, struct(*faces.shape, dtype=jnp.int32)] + packs_of(blocks) + faces_of(phases[0]),
        [hour],
        [pltpu.with_memory_space_constraint(v, pltpu.HBM) for v in (faces, right)],
        [
            pltpu.SMEM(faces.shape, jnp.int32),
            pltpu.SemaphoreType.DMA((3,)),
        ],
        vectors_in=pltpu.HBM,
    )
    faces = table
    packs = send_lanes(outs[:turns])
    early = send_faces(outs[turns:], phases[0], offsets)
    probe_right, late = turn(phases[1], kept, packs)
    stiffness = call(
        split_body, struct(headings * slots, width, 3 * width, dtype=BF16), [], [far_stiffness]
    )
    near_part = near(columns, kappa_sq, near_stiffness, probe_right)
    out = products_of(phases[0])
    own, *packs = call(
        body(early_body, phases[0]),
        [out] + packs_of(out.shape[0]),
        [hour],
        [stiffness, *early, probe_right],
    )
    packs = send_lanes(packs)
    split = SPLIT[0]
    done = late_products(phases[1][:split], late[:split], ORDER[0])
    first, image, *outs = call(
        body(middle_body, phases, heads, split),
        [field, field] + packs_of(blocks) * 2 + faces_of(heads),
        [faces, counts, hour, time_coupling],
        [near_part, own, done, stiffness, *packs, *late[split:]],
        [products_in(phases[1][split:])] + spare,
    )

    phases = PHASES[1]
    packs, first_packs = send_lanes(outs[:turns]), send_lanes(outs[turns : 2 * turns])
    early = send_faces(outs[2 * turns :], phases[0], offsets)
    near_probe = near(columns, kappa_sq, near_stiffness, image)
    near_hour, hour_image, *outgoing = call(
        body(turn_near_body, phases[1]),
        [field, field] + faces_of(phases[1]),
        [faces, hour, columns],
        [image, kappa_sq, near_stiffness, near_probe, *packs],
        near_scratch(right),
    )
    late = send_faces(outgoing, phases[1], offsets)
    own, sums = call(
        body(moments_body, phases[0]),
        [products_of(phases[0]), struct(8, lanes)],
        [faces, counts, hour],
        [probe_right, first, near_probe, stiffness, *early, *first_packs, hour_image],
    )
    sums, marks = everywhere_sum(sums)
    packs = send_lanes(
        call(
            body(repack_body),
            packs_of(own.shape[0]),
            [hour],
            [own, *marks[:1]],
        )
    )
    split = SPLIT[1]
    hour_first, partial = call(
        body(gather_body, phases, split),
        [field, field],
        [faces, counts, hour],
        [near_hour, own, first, stiffness, *first_packs, *late[:split]],
        [products_in(phases[1][:split])] + spare,
        weight=ORDER[1],
    )
    second = call(
        body(settle_body, phases, split),
        field,
        [faces, counts, hour],
        [partial, stiffness, *packs, *late[split:]],
        [products_in(phases[1][split:])] + spare,
    )
    solution_field, residual = call(
        functools.partial(close_body, len(sums)),
        [field, field],
        [],
        [right, hour_first, second, *sums],
        [pltpu.VMEM(right.shape, F32)] * 2 + [pltpu.SemaphoreType.DMA((2, PIECES))],
        outs_in=pl.ANY,
    )
    return (solution_field[None], residual[None])


def solution(mesh):
    placed = (
        P(("grp", "tm"), SPACE, None, None),
        P(("grp", "mesh", "rep"), None),
        P("grp"),
        P(SPACE, None, None),
        P(SPACE, None, None),
        P(SPACE, None),
        P(SPACE, None, None),
        P(SPACE, None),
    )
    return jax.shard_map(
        shards,
        mesh=mesh,
        in_specs=placed,
        out_specs=(
            P(("grp", "tm"), SPACE, None, None),
            P(("grp", "tm"), SPACE, None, None),
        ),
        check_vma=False,
    )
```

```python
import functools

import jax
import jax.numpy as jnp
from jax import lax
from jax.experimental import pallas as pl
from jax.experimental.pallas import tpu as pltpu
from jax.sharding import PartitionSpec as P

SPACE = ("mesh", "rep")
F32 = jnp.float32
BF16 = jnp.bfloat16
PHASES = (((4, 2), (3, 5, 1, 0)), ((2, 4, 0), (3, 5, 1)))
STAGES = (("rep", (1,)), ("tm", (1,)), ("mesh", (1, 2, 3)))
SPLIT = (3, 2)
PIECES = 8
ORDER = (40, 160, 0, 0)


def struct(*shape, dtype=F32):
    return jax.ShapeDtypeStruct(shape, dtype)


def call(
    body, outs, scalars, vectors, scratch=(), weight=0, vectors_in=pltpu.VMEM, outs_in=pltpu.VMEM
):
    spaces = [pltpu.SMEM] * len(scalars) + [vectors_in] * len(vectors)
    return pl.pallas_call(
        body,
        out_shape=outs,
        in_specs=[pl.BlockSpec(memory_space=space) for space in spaces],
        out_specs=jax.tree.map(lambda _: pl.BlockSpec(memory_space=outs_in), outs),
        scratch_shapes=scratch,
        cost_estimate=pl.CostEstimate(
            flops=(weight << 30) + 1024, transcendentals=0, bytes_accessed=1024
        ),
        compiler_params=pltpu.CompilerParams(vmem_limit_bytes=16 << 20),
    )(*scalars, *vectors)


def total(values):
    return functools.reduce(jnp.add, values)


def halves(value):
    high = value.astype(BF16)
    return high, (value - high.astype(F32)).astype(BF16)


def group_of(shape, hours):
    lanes = shape[-1]
    return lax.broadcasted_iota(jnp.int32, shape, len(shape) - 1) // (lanes // hours)


def turned(value, places, hours):
    width = value.shape[-1] // hours
    result = value
    for k in range(1, hours):
        result = jnp.where(places == k, pltpu.roll(value, k * width, value.ndim - 1), result)
    return result


def pack_lanes(hours, hour, field, outs):
    group = group_of(field.shape[1:], hours)
    for r, out in enumerate(outs):
        target = lax.rem(hour + r + 1, hours)
        for j in range(out.shape[0]):
            packed = None
            for i in range(hours):
                part = turned(field[j * hours + i], lax.rem(i - target + hours, hours), hours)
                packed = part if i == 0 else jnp.where(group == i, part, packed)
            out[j] = packed


def merge_lanes(hours, hour, own, packs, block):
    group = group_of(own.shape, hours)
    for r, pack in enumerate(packs):
        source = lax.rem(hour + hours - r - 1, hours)
        part = pack[block // hours]
        part = turned(part, lax.rem(source - block % hours + hours, hours), hours)
        own = jnp.where(group == source, part, own)
    return own


def couple(hours, coupling, value):
    lanes = value.shape[-1]
    width = lanes // hours
    before, after = (pltpu.roll(value, d, value.ndim - 1) for d in (width, lanes - width))
    if hours == 2:
        return value - coupling * before
    group = group_of(value.shape, hours)
    sides = jnp.where(group > 0, before, 0.0) + jnp.where(group < hours - 1, after, 0.0)
    return value - coupling * sides


def pack_faces(faces, field, headings, outs):
    slots = faces.shape[1]
    places = [out.at[k] for out in outs for k in range(out.shape[0])]
    for m, place in enumerate(places):
        place[...] = field[faces[0, m % slots, headings[m // slots]]]


def far_product(stiffness, q, block):
    high, low = halves(block)
    right = jnp.concatenate([high, high, low], axis=0)
    return jnp.dot(stiffness[q], right, preferred_element_type=F32)


def landing(faces, counts, e, f, spare):
    return jnp.where(f < counts[0, e], faces[0, f, e], spare)


def open_body(hours, heads, hour, faces_in, field_in, *refs):
    (field, table, *outs), (faces, sems) = refs[:-2], refs[-2:]
    copies = [
        pltpu.make_async_copy(field_in, field, sems.at[0]),
        pltpu.make_async_copy(faces_in, faces, sems.at[1]),
        pltpu.make_async_copy(faces_in, table, sems.at[2]),
    ]
    for copy in copies:
        copy.start()
    copies[0].wait()
    pack_lanes(hours, hour[0], field, outs[: hours - 1])
    copies[1].wait()
    pack_faces(faces, field, heads, outs[hours - 1 :])
    copies[2].wait()


def turn_body(hours, heads, faces, hour, field, *refs):
    packs, (out, *faces_out) = refs[: hours - 1], refs[hours - 1 :]
    for b in range(field.shape[0]):
        out[b] = merge_lanes(hours, hour[0], field[b], packs, b)
    pack_faces(faces, out, heads, faces_out)


def turn_near_body(hours, heads, faces, hour, columns, field, kappa, stiffness, _, *refs):
    packs, (near_out, *outs) = refs[: hours - 1], refs[hours - 1 :]
    outs, scratch = outs[: 1 + len(heads)], outs[1 + len(heads) :]
    turn_body(hours, heads, faces, hour, field, *packs, *outs)
    near_body(columns, kappa, stiffness, outs[0], near_out, *scratch)


def split_body(stiffness, out):
    width = stiffness.shape[1]
    for q in range(out.shape[0]):
        high, low = halves(stiffness[0, :, q * width : (q + 1) * width])
        out[q] = jnp.concatenate([high, low, high], axis=1)


def near_body(columns, kappa, stiffness, field, out, high, low, diagonal):
    blocks = field.shape[0]
    slots = columns.shape[0]
    diagonal[...] = jnp.transpose(kappa[...])
    for b in range(blocks):
        high[b], low[b] = halves(field[b])
    for b in range(blocks):
        index = [columns[k, b] for k in range(slots)]
        highs = jnp.concatenate([high[i] for i in index], axis=0)
        lows = jnp.concatenate([low[i] for i in index], axis=0)
        left_high, left_low = halves(stiffness[b])
        value = jnp.dot(left_high, highs, preferred_element_type=F32)
        value += jnp.dot(left_low, highs, preferred_element_type=F32)
        value += jnp.dot(left_high, lows, preferred_element_type=F32)
        out[b] = value + (3.0 + diagonal[:, b : b + 1]) * field[b]


def near_scratch(field):
    blocks, width, lanes = field.shape
    return [pltpu.VMEM(field.shape, BF16)] * 2 + [pltpu.VMEM((width, blocks), F32)]


def near(columns, kappa, stiffness, field):
    return call(
        near_body,
        struct(*field.shape),
        [columns],
        [kappa, stiffness, field],
        near_scratch(field),
    )


def products(heads, stiffness, arrived, out):
    for n, e in enumerate(heads):
        slots = arrived[n].shape[0]
        for f in range(slots):
            out[n * slots + f] = far_product(stiffness, (e ^ 1) * slots + f, arrived[n][f])


def early_body(hours, heads, hour, stiffness, *refs):
    arrived, (_, out, *packs) = refs[: len(heads)], refs[len(heads) :]
    products(heads, stiffness, arrived, out)
    pack_lanes(hours, hour[0], out, packs)


def repack_body(hours, hour, own, *refs):
    pack_lanes(hours, hour[0], own, refs[1 - hours :])


def sum_body(*refs):
    refs[-1][...] = refs[-2][...] = total([ref[...] for ref in refs[:-2]])


def late_body(heads, stiffness, *refs):
    products(heads, stiffness, refs[:-1], refs[-1])


def gather_far(hours, phases, faces, counts, hour, own, packs, late, near_part, field):
    blocks = near_part.shape[0]
    slots = faces.shape[1]
    for b in range(blocks):
        field[b] = near_part[b]
    for part, heads in enumerate(phases):
        for n, e in enumerate(heads):
            for f in range(slots):
                q = n * slots + f
                value = late(q) if part else merge_lanes(hours, hour[0], own[q], packs, q)
                field[landing(faces, counts, e ^ 1, f, blocks)] += value


def late_values(phases, done, stiffness, arrived, rest):
    count = done.shape[0]
    products(phases[1][len(phases[1]) - len(arrived) :], stiffness, arrived, rest)
    return lambda q: done[q] if q < count else rest[q - count]


def middle_body(
    hours, phases, heads, split, faces, counts, hour, coupling, near_part, own, done, stiffness, *refs
):
    turns = hours - 1
    packs, refs = refs[:turns], refs[turns:]
    left = len(phases[1]) - split
    arrived, (first, image, *outs, rest, field) = refs[:left], refs[left:]
    image_packs, first_packs, faces_out = outs[:turns], outs[turns : 2 * turns], outs[2 * turns :]
    late = late_values(phases, done, stiffness, arrived, rest)
    gather_far(hours, phases, faces, counts, hour, own, packs, late, near_part, field)
    for b in range(first.shape[0]):
        once = couple(hours, coupling[0], field[b])
        first[b] = once
        image[b] = couple(hours, coupling[0], once)
    pack_lanes(hours, hour[0], image, image_packs)
    pack_faces(faces, image, heads, faces_out)
    pack_lanes(hours, hour[0], first, first_packs)


def moments_body(hours, heads, faces, counts, hour, right, first, second, stiffness, *refs):
    arrived, (own, out) = refs[: len(heads)], refs[-2:]
    products(heads, stiffness, arrived, own)
    slots = faces.shape[1]
    sums = [jnp.zeros(right.shape[1:], F32) for _ in range(4)]
    for b in range(right.shape[0]):
        start, image = right[b], first[b]
        sums[0] += start * start
        sums[1] += start * image
        sums[2] += image * image
        sums[3] += image * second[b]
    for n, e in enumerate(heads):
        for f in range(slots):
            weight = jnp.where(f < counts[0, e ^ 1], 2.0, 0.0)
            sums[3] += weight * (first[faces[0, f, e ^ 1]] * own[n * slots + f])
    rows = jnp.concatenate([jnp.sum(s, axis=0, keepdims=True) for s in sums] * 2, axis=0)
    width = rows.shape[1] // hours
    rows = total([rows] + [pltpu.roll(rows, k * width, 1) for k in range(1, hours)])
    out[...] = jnp.where(group_of(rows.shape, hours) == hour[0], rows, 0.0)


def gather_body(
    hours, phases, split, faces, counts, hour, near_part, own, first, stiffness, *refs
):
    turns = hours - 1
    first_packs, refs = refs[:turns], refs[turns:]
    arrived, (image, out, made, field) = refs[:split], refs[split:]
    blocks, slots = first.shape[0], faces.shape[1]
    heads = phases[1][:split]
    products(heads, stiffness, arrived, made)
    for b in range(blocks):
        image[b] = merge_lanes(hours, hour[0], first[b], first_packs, b)
        field[b] = near_part[b]
    mine = group_of(own.shape[1:], hours) == hour[0]
    for n, e in enumerate(phases[0]):
        for f in range(slots):
            block = landing(faces, counts, e ^ 1, f, blocks)
            field[block] += jnp.where(mine, own[n * slots + f], 0.0)
    for n, e in enumerate(heads):
        for f in range(slots):
            field[landing(faces, counts, e ^ 1, f, blocks)] += made[n * slots + f]
    for b in range(blocks):
        out[b] = field[b]


def settle_body(hours, phases, split, faces, counts, hour, start, stiffness, *refs):
    turns = hours - 1
    packs, refs = refs[:turns], refs[turns:]
    arrived, (out, made, field) = refs[:-3], refs[-3:]
    blocks, slots = start.shape[0], faces.shape[1]
    heads = phases[1][split:]
    products(heads, stiffness, arrived, made)
    for b in range(blocks):
        field[b] = start[b]
    zero = jnp.zeros(start.shape[1:], F32)
    for n, e in enumerate(phases[0]):
        for f in range(slots):
            value = merge_lanes(hours, hour[0], zero, packs, n * slots + f)
            field[landing(faces, counts, e ^ 1, f, blocks)] += value
    for n, e in enumerate(heads):
        for f in range(slots):
            field[landing(faces, counts, e ^ 1, f, blocks)] += made[n * slots + f]
    for b in range(blocks):
        out[b] = field[b]


def close_body(parts, right, first, second, *refs):
    sums, (solution, residual, solved, left, sems) = refs[:parts], refs[parts:]
    moment = total([s[...] for s in sums])
    m0, m1, m2, m3 = (moment[k : k + 1] for k in range(4))
    alpha = m0 / m1
    norm = alpha * alpha * m2 - m0
    lift = 1.0 + norm / m0
    step = norm / (lift * lift * m1 - 2.0 * lift * alpha * m2 + alpha * alpha * m3)
    on_right = alpha + step * lift
    on_first = step * alpha
    pieces = sems.shape[1]
    size = right.shape[0] // pieces
    copies = []
    for p in range(pieces):
        part = pl.ds(p * size, size)
        for b in range(p * size, (p + 1) * size):
            start, image = right[b], first[b]
            solved[b] = on_right * start - on_first * image
            left[b] = start - on_right * image + on_first * second[b]
        for n, (source, target) in enumerate(((solved, solution), (left, residual))):
            copies.append(pltpu.make_async_copy(source.at[part], target.at[part], sems.at[n, p]))
            copies[-1].start()
    for copy in copies:
        copy.wait()


def shifted(value, axes, sizes, steps):
    route = []
    for source in range(functools.reduce(lambda a, b: a * b, sizes)):
        rest, target, scale = source, 0, 1
        for size, step in reversed(list(zip(sizes, steps))):
            rest, place = divmod(rest, size)
            target += (place + step) % size * scale
            scale *= size
        route.append((source, target))
    return lax.ppermute(value, axes, route)


def send_faces(outgoing, heads, offsets):
    count = lax.axis_size(SPACE)
    return [shifted(v, SPACE, (count,), (offsets[e],)) for v, e in zip(outgoing, heads)]


def send_lanes(packs):
    hours = lax.axis_size("tm")
    return [shifted(v, ("tm",), (hours,), (r + 1,)) for r, v in enumerate(packs)]


def everywhere_sum(value):
    terms, summed, marks = [value], [], []
    for axis, partners in STAGES:
        if axis in summed:
            continue
        if len(terms) > 1:
            weight = ORDER[2 + len(marks)]
            sent, kept = call(sum_body, [struct(*value.shape)] * 2, [], terms, weight=weight)
            terms = [kept]
            marks += terms
        else:
            sent = value
        count = lax.axis_size(axis)
        if count in (2, 4):
            routes = [[(i, i ^ k) for i in range(count)] for k in partners]
            terms += [lax.ppermute(sent, axis, route) for route in routes]
        else:
            terms = [lax.psum(sent, axis)]
            summed.append(axis)
    return terms, marks


def shards(
    right_side,
    kappa_sq,
    time_coupling,
    near_stiffness,
    far_stiffness,
    near_columns,
    face_blocks,
    face_counts,
):
    right = right_side.reshape(right_side.shape[1:])
    blocks, width, lanes = right.shape
    hours = lax.axis_size("tm")
    hour = lax.axis_index("tm").reshape(1)
    headings, slots = face_blocks.shape[1:]
    stride = lax.axis_size(SPACE) // 4 + 1
    faces = jnp.swapaxes(face_blocks, 1, 2)
    columns = jnp.swapaxes(near_columns, 0, 1)
    counts = face_counts
    offsets = (1, -1, 2, -2, stride, -stride)
    field = struct(*right.shape)
    turns = hours - 1
    spare = [pltpu.VMEM((blocks + 1, width, lanes), F32)]

    def packs_of(count):
        return [struct(count // hours, width, lanes)] * turns

    def faces_of(heads):
        return [struct(slots, width, lanes)] * len(heads)

    def products_of(heads):
        return struct(len(heads) * slots, width, lanes)

    def products_in(heads):
        return pltpu.VMEM((max(len(heads), 1) * slots, width, lanes), F32)

    def body(function, *sizes):
        return functools.partial(function, hours, *sizes)

    def turn(heads, field_in, packs):
        out, *outgoing = call(
            body(turn_body, heads), [field] + faces_of(heads), [faces, hour], [field_in, *packs]
        )
        return out, send_faces(outgoing, heads, offsets)

    def late_products(heads, arrived, weight):
        return call(
            functools.partial(late_body, heads),
            products_of(heads),
            [],
            [stiffness, *arrived],
            weight=weight,
        )

    phases, (heads, _) = PHASES
    kept, table, *outs = call(
        body(open_body, phases[0]),
        [field, struct(*faces.shape, dtype=jnp.int32)] + packs_of(blocks) + faces_of(phases[0]),
        [hour],
        [pltpu.with_memory_space_constraint(v, pltpu.HBM) for v in (faces, right)],
        [
            pltpu.SMEM(faces.shape, jnp.int32),
            pltpu.SemaphoreType.DMA((3,)),
        ],
        vectors_in=pltpu.HBM,
    )
    faces = table
    packs = send_lanes(outs[:turns])
    early = send_faces(outs[turns:], phases[0], offsets)
    probe_right, late = turn(phases[1], kept, packs)
    stiffness = call(
        split_body, struct(headings * slots, width, 3 * width, dtype=BF16), [], [far_stiffness]
    )
    near_part = near(columns, kappa_sq, near_stiffness, probe_right)
    out = products_of(phases[0])
    own, *packs = call(
        body(early_body, phases[0]),
        [out] + packs_of(out.shape[0]),
        [hour],
        [stiffness, *early, probe_right],
    )
    packs = send_lanes(packs)
    split = SPLIT[0]
    done = late_products(phases[1][:split], late[:split], ORDER[0])
    first, image, *outs = call(
        body(middle_body, phases, heads, split),
        [field, field] + packs_of(blocks) * 2 + faces_of(heads),
        [faces, counts, hour, time_coupling],
        [near_part, own, done, stiffness, *packs, *late[split:]],
        [products_in(phases[1][split:])] + spare,
    )

    phases = PHASES[1]
    packs, first_packs = send_lanes(outs[:turns]), send_lanes(outs[turns : 2 * turns])
    early = send_faces(outs[2 * turns :], phases[0], offsets)
    near_probe = near(columns, kappa_sq, near_stiffness, image)
    near_hour, hour_image, *outgoing = call(
        body(turn_near_body, phases[1]),
        [field, field] + faces_of(phases[1]),
        [faces, hour, columns],
        [image, kappa_sq, near_stiffness, near_probe, *packs],
        near_scratch(right),
    )
    late = send_faces(outgoing, phases[1], offsets)
    own, sums = call(
        body(moments_body, phases[0]),
        [products_of(phases[0]), struct(8, lanes)],
        [faces, counts, hour],
        [probe_right, first, near_probe, stiffness, *early, *first_packs, hour_image],
    )
    sums, marks = everywhere_sum(sums)
    packs = send_lanes(
        call(
            body(repack_body),
            packs_of(own.shape[0]),
            [hour],
            [own, *marks[:1]],
        )
    )
    split = SPLIT[1]
    hour_first, partial = call(
        body(gather_body, phases, split),
        [field, field],
        [faces, counts, hour],
        [near_hour, own, first, stiffness, *first_packs, *late[:split]],
        [products_in(phases[1][:split])] + spare,
        weight=ORDER[1],
    )
    second = call(
        body(settle_body, phases, split),
        field,
        [faces, counts, hour],
        [partial, stiffness, *packs, *late[split:]],
        [products_in(phases[1][split:])] + spare,
    )
    solution_field, residual = call(
        functools.partial(close_body, len(sums)),
        [field, field],
        [],
        [right, hour_first, second, *sums],
        [pltpu.VMEM(right.shape, F32)] * 2 + [pltpu.SemaphoreType.DMA((2, PIECES))],
        outs_in=pl.ANY,
    )
    return (solution_field[None], residual[None])


def solution(mesh):
    placed = (
        P(("grp", "tm"), SPACE, None, None),
        P(("grp", "mesh", "rep"), None),
        P("grp"),
        P(SPACE, None, None),
        P(SPACE, None, None),
        P(SPACE, None),
        P(SPACE, None, None),
        P(SPACE, None),
    )
    return jax.shard_map(
        shards,
        mesh=mesh,
        in_specs=placed,
        out_specs=(
            P(("grp", "tm"), SPACE, None, None),
            P(("grp", "tm"), SPACE, None, None),
        ),
        check_vma=False,
    )
```
